256 devices in a mesh: tm: 8 (over x, core), pair: 32 (over z, y).
Axes of the slice: x: 4, y: 4, z: 8, core: 2. Of those that a mesh axis runs over, the one named last changes fastest.
Arguments:
- mode_fields: bfloat16 [2, 256, 4096], P(None, None, 'tm'), may hold values from -6 to 6
- raman_taps: bfloat16 [128], replicated, may hold values from -0.5 to 0.5
- pair_blocks: int32 [32, 16, 2], P('pair'), may hold values from 0 to 31
- light_blocks: int32 [32, 16, 2], P('pair'), may hold values from 0 to 31
- target_blocks: int32 [1024, 1], P('pair'), may hold values from 0 to 31; in each aligned block of 32 rows (0 to 31, 32 to 63, ...) at most 2 rows name the same one
- raman_values: bfloat16 [32, 16, 2, 4096], P('pair'), may hold values from -0.03125 to 0.03125
- live_slots: int32 [32], P('pair'), may hold values from 11 to 16, as said below
Outputs:
- raman_term: float32 [2, 256, 4096], P(None, 'pair', 'tm')
The draws below stay inside these ranges and needn't reach their ends.
Inputs may be any that keep to these rules, and one draw needn't show every extreme that they name: `target_blocks`: within the 32 rows of one index of pair, no mode block is named by more than 2 rows, a bound that some block reaches. `live_slots`: some index of pair uses all 16 slots in every draw; every index uses at least 11.
All inputs are finite; a program needn't handle non-finite values.
Results may differ from the reference program's by a relative error of at most 0.004.
Values may be sent and summed in bfloat16 or wider, within the bound.
A program may use at most 64 MiB of HBM per device.

```python
import math
import jax
import jax.numpy as jnp
import numpy as np
from jax import lax

M = 256
MB = 8
NB = 32
NT = 4096
HL = 128
PB = 16
KB = 2
CAPB = 2
N_PAIR = 32


def draw_live_slots(key, part):
    key_counts, key_fullest = jax.random.split(jax.random.fold_in(key, 11))
    live_draw = jax.random.randint(key_counts, (N_PAIR,), PB - PB // 3, PB + 1)
    fullest = jax.random.randint(key_fullest, (), 0, N_PAIR)
    return jnp.where(jnp.arange(N_PAIR) == fullest, PB, live_draw).astype(jnp.int32)


def set_ends(values, stream_key, smallest, high):
    dims = values.shape
    place = [jax.random.randint(jax.random.fold_in(stream_key, axis), (), 0, dims[axis]) for axis in range(len(dims))]
    values = values.at[tuple(place)].set(smallest)
    longest = dims.index(max(dims))
    place[longest] = (place[longest] + 1) % dims[longest]
    return values.at[tuple(place)].set(high)


def shard_levels(own_key, shape, shards, smallest, high):
    def one(position, shards_of):
        heights = jax.random.uniform(jax.random.fold_in(jax.random.fold_in(own_key, 6), position), (shards_of,), jnp.float32, smallest / len(shards), high / len(shards))
        return jnp.repeat(jnp.exp(heights), shape[position] // shards_of).reshape((-1,) + (1,) * (len(shape) - position - 1))

    gain = one(*shards[0])
    for cut in shards[1:]:
        gain = gain * one(*cut)
    return gain


def shared_out(rng, own, number, rows, count, top, most, skew):
    ranking = jax.random.permutation(rng, count)
    heavy_load, common = load_shares(count, rows * top, most, skew, True), load_shares(count, rows * top, most, skew, False)
    places = jnp.arange(count)

    def named(lengths, rotation):
        used = int((lengths > 0).sum())
        fixed = max(1, used // 4)
        shifted = fixed + (places - fixed + rotation * (used - fixed)) % max(1, count - fixed)
        return jnp.zeros((count,), jnp.int32).at[ranking[jnp.where(places < fixed, places, shifted)]].set(jnp.asarray(lengths, jnp.int32))

    lengths = jnp.where(number % 4 == 0, named(heavy_load, number // 4), named(common, number - number // 4 - 1))
    mixed = jax.random.permutation(jax.random.fold_in(own, 3), count)
    donor, sink = mixed[0:count // 2 * 2:2], mixed[1:count // 2 * 2:2]
    slack = jnp.minimum(lengths[donor] - 1, most - lengths[sink]) // 2
    slack = jnp.where((donor == ranking[0]) | (sink == ranking[0]) | (lengths[sink] == 0), 0, jnp.maximum(slack, 0))
    shifted = jax.random.randint(jax.random.fold_in(own, 4), (count // 2,), 0, 1 << 20) % (slack + 1)
    lengths = lengths.at[donor].add(-shifted).at[sink].add(shifted)
    members = jnp.searchsorted(jnp.cumsum(lengths), jnp.arange(rows * top), side="right").astype(jnp.int32)
    grid = members.reshape(top, rows).T
    grid = grid[jax.random.permutation(jax.random.fold_in(own, 1), rows)]
    rotation = jax.random.randint(jax.random.fold_in(own, 2), (rows, 1), 0, top)
    return jnp.take_along_axis(grid, (jnp.arange(top)[None, :] + rotation) % top, axis=1)


def load_shares(amount, total, limit, skew, full):
    weights = [(1 << 20) // math.isqrt(standing ** skew) + 1 for standing in range(1, amount + 1)]
    largest = limit if full else min(limit, max(-(-total // amount), total * weights[0] // sum(weights)))
    least = 1 if total - largest >= amount - 1 else 0
    given, surplus = [largest] + [least] * (amount - 1), total - largest - least * (amount - 1)
    while surplus > 0:
        candidates = [i for i in range(1, amount) if given[i] < largest] or [i for i in range(1, amount) if given[i] < limit]
        whole, budget = sum([weights[i] for i in candidates]), surplus
        for i in candidates:
            addition = min(limit - given[i], max(1, budget * weights[i] // whole), surplus)
            given[i] = given[i] + addition
            surplus = surplus - addition
    return np.array(given)


def gaussian(key, shape, deviation, bound, cuts=(), kind=jnp.bfloat16):
    values = jax.random.normal(key, shape, jnp.float32) * deviation
    if len(cuts) > 0:
        values = shard_levels(key, shape, cuts, -0.22, 0.18) * values
    return jnp.clip(values, min=-bound, max=bound).astype(kind)


def setup_inputs(seed: int = 0) -> dict:
    arg_keys = jax.random.split(jax.random.key(seed), 8)
    mode_fields = gaussian(arg_keys[0], (2, M, NT), 1.0, 6.0, ((2, 8),))
    raman_taps = gaussian(arg_keys[1], (HL,), HL ** -0.5, 0.5)
    pair_blocks = set_ends(jax.random.randint(arg_keys[2], (N_PAIR, PB, 2), 0, NB), jax.random.fold_in(arg_keys[2], 1), 0, NB - 1).astype(jnp.int32)
    light_blocks = set_ends(jax.random.randint(arg_keys[3], (N_PAIR, PB, KB), 0, NB), jax.random.fold_in(arg_keys[3], 1), 0, NB - 1).astype(jnp.int32)
    target_blocks_keys = jax.random.split(jax.random.fold_in(arg_keys[4], 1), (N_PAIR * PB * KB) // (PB * KB))
    target_blocks_turns = jax.random.permutation(jax.random.fold_in(arg_keys[4], 3), (N_PAIR * PB * KB) // (PB * KB))
    target_blocks = jax.vmap(lambda own, number: shared_out(jax.random.fold_in(arg_keys[4], 2), own, number, PB * KB, NB, 1, CAPB, 2))(target_blocks_keys, target_blocks_turns).reshape((N_PAIR * PB * KB, 1))
    raman_values = gaussian(arg_keys[5], (N_PAIR, PB, KB, MB * MB * MB * MB), (MB ** 5) ** -0.5, 0.03125, ((0, 32),))
    live_slots = draw_live_slots(jax.random.fold_in(arg_keys[7], 71), 0)
    return {"mode_fields": mode_fields, "raman_taps": raman_taps, "pair_blocks": pair_blocks, "light_blocks": light_blocks, "target_blocks": target_blocks, "raman_values": raman_values, "live_slots": live_slots}


def toeplitz_table(tap_values):
    tap_count = tap_values.shape[0]
    row_index = jnp.arange(2 * tap_count, dtype=jnp.int32)[:, None]
    col_index = jnp.arange(tap_count, dtype=jnp.int32)[None, :]
    lag_index = tap_count + col_index - row_index
    tap_index = jnp.clip(lag_index - 1, 0, tap_count - 1)
    chosen = jnp.take(tap_values, tap_index)
    return jnp.where((lag_index >= 1) & (lag_index <= tap_count), chosen, jnp.zeros_like(chosen))


def delayed(signal, toeplitz):
    tap_count = toeplitz.shape[1]
    out_length = signal.shape[1] - tap_count
    block_total = out_length // tap_count
    row_total = signal.shape[0]
    pieces = signal.reshape(row_total, block_total + 1, tap_count)
    windows = jnp.concatenate([pieces[:, :-1], pieces[:, 1:]], axis=2)
    flat_windows = windows.reshape(row_total * block_total, 2 * tap_count)
    result = jnp.dot(flat_windows, toeplitz, preferred_element_type=jnp.float32)
    return result.reshape(row_total, out_length)


def block_rows(fields, target, block_size):
    return lax.dynamic_slice_in_dim(fields, target * block_size, block_size, 1)


def slot_partials(window, pair_ids, light_ids, values, toeplitz, block_size):
    tap_count = toeplitz.shape[1]
    length = window.shape[2] - tap_count
    square = block_size * block_size
    left_field = block_rows(window, pair_ids[0], block_size).astype(jnp.float32)
    right_field = block_rows(window, pair_ids[1], block_size).astype(jnp.float32)
    real_part = (left_field[0][:, None] * right_field[0][None] + left_field[1][:, None] * right_field[1][None]).reshape(square, -1)
    imag_part = (left_field[1][:, None] * right_field[0][None] - left_field[0][:, None] * right_field[1][None]).reshape(square, -1)
    intensity = jnp.concatenate([real_part, imag_part], 0).astype(jnp.bfloat16)
    response = delayed(intensity, toeplitz).astype(jnp.bfloat16)
    partials = []
    for entry_index in range(values.shape[0]):
        matrix = values[entry_index].reshape(square, square)
        mixed_real = jnp.dot(matrix, response[:square], preferred_element_type=jnp.float32).reshape(block_size, block_size, length)
        mixed_imag = jnp.dot(matrix, response[square:], preferred_element_type=jnp.float32).reshape(block_size, block_size, length)
        light_field = block_rows(window, light_ids[entry_index], block_size)[:, :, tap_count:].astype(jnp.float32)
        out_real = jnp.sum(light_field[0][None] * mixed_real - light_field[1][None] * mixed_imag, axis=1)
        out_imag = jnp.sum(light_field[0][None] * mixed_imag + light_field[1][None] * mixed_real, axis=1)
        partials.append(jnp.stack([out_real, out_imag]))
    return partials


def reference(mode_fields, raman_taps, pair_blocks, light_blocks, target_blocks, raman_values, live_slots):
    toeplitz = toeplitz_table(raman_taps)
    window = jnp.concatenate([jnp.zeros((2, M, HL), jnp.bfloat16), mode_fields], 2)
    targets = target_blocks.reshape(N_PAIR, PB, KB)
    totals = jnp.zeros((2, M, NT), jnp.float32)

    def scan_step(totals, flat_index):
        owner_index = flat_index // PB
        slot_index = flat_index % PB

        def add_slot(totals):
            partials = slot_partials(window, pair_blocks[owner_index, slot_index], light_blocks[owner_index, slot_index], raman_values[owner_index, slot_index], toeplitz, MB)
            for entry_index in range(KB):
                target = targets[owner_index, slot_index, entry_index]
                current = lax.dynamic_slice_in_dim(totals, target * MB, MB, 1)
                totals = lax.dynamic_update_slice_in_dim(totals, current + partials[entry_index], target * MB, 1)
            return totals

        def keep_slot(totals):
            return totals

        totals = lax.cond(slot_index < live_slots[owner_index], add_slot, keep_slot, totals)
        return totals, None

    totals, _ = lax.scan(scan_step, totals, jnp.arange(N_PAIR * PB, dtype=jnp.int32))
    return totals
```

```python
import jax
import jax.numpy as jnp
from jax import lax
from jax.sharding import PartitionSpec as P

MB = 8


def toeplitz_table(tap_values):
    tap_count = tap_values.shape[0]
    rows = 2 * tap_count
    period = rows + tap_count
    zeros = jnp.zeros((rows,), tap_values.dtype)
    base = jnp.concatenate([tap_values[tap_count - 1:], zeros, tap_values[: tap_count - 1]])
    tiled = jnp.tile(base, rows)[: rows * (period - 1)].reshape(rows, period - 1)
    return tiled[:, :tap_count]


def delayed(signal, toeplitz):
    tap_count = toeplitz.shape[1]
    out_length = signal.shape[1] - tap_count
    block_total = out_length // tap_count
    row_total = signal.shape[0]
    pieces = signal.reshape(row_total, block_total + 1, tap_count)
    windows = jnp.concatenate([pieces[:, :-1], pieces[:, 1:]], axis=2)
    flat_windows = windows.reshape(row_total * block_total, 2 * tap_count)
    result = jnp.dot(flat_windows, toeplitz, preferred_element_type=jnp.float32)
    return result.reshape(row_total, out_length)


def slot_partials(blocked, pair_ids, light_ids, values, toeplitz):
    tap_count = toeplitz.shape[1]
    block_size = blocked.shape[2]
    length = blocked.shape[3] - tap_count
    square = block_size * block_size
    left_field = blocked[pair_ids[0]]
    right_field = blocked[pair_ids[1]]
    left_real = left_field[0].astype(jnp.float32)[:, None]
    left_imag = left_field[1].astype(jnp.float32)[:, None]
    right_real = right_field[0].astype(jnp.float32)[None]
    right_imag = right_field[1].astype(jnp.float32)[None]
    real_part = (left_real * right_real + left_imag * right_imag).reshape(square, -1)
    imag_part = (left_imag * right_real - left_real * right_imag).reshape(square, -1)
    intensity = jnp.concatenate([real_part, imag_part], 0).astype(jnp.bfloat16)
    response = delayed(intensity, toeplitz).astype(jnp.bfloat16)
    partials = []
    for entry_index in range(values.shape[0]):
        matrix = values[entry_index].reshape(square, square)
        mixed_real = jnp.dot(matrix, response[:square], preferred_element_type=jnp.float32).reshape(
            block_size, block_size, length
        )
        mixed_imag = jnp.dot(matrix, response[square:], preferred_element_type=jnp.float32).reshape(
            block_size, block_size, length
        )
        light_field = blocked[light_ids[entry_index]][:, :, tap_count:]
        light_real = light_field[0][None]
        light_imag = light_field[1][None]
        out_real = jnp.sum(
            light_real.astype(jnp.float32) * mixed_real
            - light_imag.astype(jnp.float32) * mixed_imag,
            axis=1,
        )
        out_imag = jnp.sum(
            light_real.astype(jnp.float32) * mixed_imag
            + light_imag.astype(jnp.float32) * mixed_real,
            axis=1,
        )
        partials.append(jnp.stack([out_real, out_imag]))
    return partials


def local(
    mode_fields, raman_taps, pair_blocks, light_blocks, target_blocks, raman_values, live_slots
):
    toeplitz = toeplitz_table(raman_taps)
    tap_count = toeplitz.shape[1]
    block_size = MB
    tm_count = lax.axis_size("tm")
    pair_count = lax.axis_size("pair")
    slot_count = pair_blocks.shape[1]
    entries = light_blocks.shape[2]
    mode_count = mode_fields.shape[1]
    blocks = mode_count // block_size
    live_count = live_slots[0]
    targets = target_blocks.reshape(slot_count, entries)
    halo = lax.ppermute(
        mode_fields[:, :, -tap_count:], "tm", [(k, k + 1) for k in range(tm_count - 1)]
    )
    window = jnp.concatenate([halo, mode_fields], 2)
    full_length = window.shape[2]
    length = full_length - tap_count
    blocked = jnp.transpose(window.reshape(2, blocks, block_size, full_length), (1, 0, 2, 3))
    buffers = jnp.zeros((blocks, 2, block_size, length), jnp.float32)

    def one_slot(slot_index, buffers):
        partials = slot_partials(
            blocked,
            pair_blocks[0, slot_index],
            light_blocks[0, slot_index],
            raman_values[0, slot_index],
            toeplitz,
        )
        for entry_index in range(entries):
            target = targets[slot_index, entry_index]
            current = lax.dynamic_index_in_dim(buffers, target, 0, True)
            buffers = lax.dynamic_update_index_in_dim(
                buffers, current + partials[entry_index][None], target, 0
            )
        return buffers

    turn_count = jnp.clip(live_count, 0, slot_count)
    buffers = lax.fori_loop(0, turn_count, one_slot, buffers)
    owned = blocks // pair_count
    received = lax.all_to_all(buffers, "pair", split_axis=0, concat_axis=0, tiled=True)
    shared = received.reshape(pair_count, owned, 2, block_size, length).sum(axis=0)
    result = jnp.transpose(shared, (1, 0, 2, 3)).reshape(2, owned * block_size, length)
    return result


def solution(mesh):
    return jax.shard_map(
        local,
        mesh=mesh,
        in_specs=(
            P(None, None, "tm"),
            P(),
            P("pair", None, None),
            P("pair", None, None),
            P("pair", None),
            P("pair", None, None, None),
            P("pair"),
        ),
        out_specs=P(None, "pair", "tm"),
        check_vma=False,
    )
```

```python
import jax
import jax.numpy as jnp
from jax import lax
from jax.sharding import PartitionSpec as P
from jax.experimental import pallas as pl
from jax.experimental.pallas import tpu as pltpu

MB = 8


def toeplitz_table(tap_values):
    tap_count = tap_values.shape[0]
    rows = 2 * tap_count
    period = rows + tap_count
    zeros = jnp.zeros((rows,), tap_values.dtype)
    base = jnp.concatenate([tap_values[tap_count - 1:], zeros, tap_values[: tap_count - 1]])
    tiled = jnp.tile(base, rows)[: rows * (period - 1)].reshape(rows, period - 1)
    return tiled[:, :tap_count]


def delayed(signal, toeplitz):
    tap_count = toeplitz.shape[1]
    out_length = signal.shape[1] - tap_count
    block_total = out_length // tap_count
    row_total = signal.shape[0]
    pieces = signal.reshape(row_total, block_total + 1, tap_count)
    windows = jnp.concatenate([pieces[:, :-1], pieces[:, 1:]], axis=2)
    flat_windows = windows.reshape(row_total * block_total, 2 * tap_count)
    result = jnp.dot(flat_windows, toeplitz, preferred_element_type=jnp.float32)
    return result.reshape(row_total, out_length)


def slot_partials(blocked, pair_ids, light_ids, values, toeplitz):
    tap_count = toeplitz.shape[1]
    block_size = blocked.shape[2]
    length = blocked.shape[3] - tap_count
    square = block_size * block_size
    left_field = blocked[pair_ids[0]]
    right_field = blocked[pair_ids[1]]
    left_real = left_field[0].astype(jnp.float32)[:, None]
    left_imag = left_field[1].astype(jnp.float32)[:, None]
    right_real = right_field[0].astype(jnp.float32)[None]
    right_imag = right_field[1].astype(jnp.float32)[None]
    real_part = (left_real * right_real + left_imag * right_imag).reshape(square, -1)
    imag_part = (left_imag * right_real - left_real * right_imag).reshape(square, -1)
    intensity = jnp.concatenate([real_part, imag_part], 0).astype(jnp.bfloat16)
    response = delayed(intensity, toeplitz).astype(jnp.bfloat16)
    partials = []
    for entry_index in range(values.shape[0]):
        matrix = values[entry_index].reshape(square, square)
        mixed_real = jnp.dot(matrix, response[:square], preferred_element_type=jnp.float32).reshape(
            block_size, block_size, length
        )
        mixed_imag = jnp.dot(matrix, response[square:], preferred_element_type=jnp.float32).reshape(
            block_size, block_size, length
        )
        light_field = blocked[light_ids[entry_index]][:, :, tap_count:]
        light_real = light_field[0][None]
        light_imag = light_field[1][None]
        out_real = jnp.sum(
            light_real.astype(jnp.float32) * mixed_real
            - light_imag.astype(jnp.float32) * mixed_imag,
            axis=1,
        )
        out_imag = jnp.sum(
            light_real.astype(jnp.float32) * mixed_imag
            + light_imag.astype(jnp.float32) * mixed_real,
            axis=1,
        )
        partials.append(jnp.stack([out_real, out_imag]))
    return partials


def slot_kernel(pairs_ref, lights_ref, targets_ref, live_ref, fields_ref, table_ref, values_ref, out_ref):
    block_size = fields_ref.shape[2]
    width = fields_ref.shape[3]
    length = out_ref.shape[3]
    tap_count = width - length
    square = block_size * block_size
    entries = values_ref.shape[1]
    slot_count = values_ref.shape[0]
    out_ref[...] = jnp.zeros(out_ref.shape, out_ref.dtype)
    table = table_ref[...]

    def body(slot_index, carry):
        left = pairs_ref[2 * slot_index]
        right = pairs_ref[2 * slot_index + 1]
        left_real = fields_ref[0, left].astype(jnp.float32)[:, None]
        left_imag = fields_ref[1, left].astype(jnp.float32)[:, None]
        right_real = fields_ref[0, right].astype(jnp.float32)[None]
        right_imag = fields_ref[1, right].astype(jnp.float32)[None]
        real_part = (left_real * right_real + left_imag * right_imag).reshape(square, width)
        imag_part = (left_imag * right_real - left_real * right_imag).reshape(square, width)
        intensity = jnp.concatenate([real_part, imag_part], 0).astype(jnp.bfloat16)
        pieces = []
        for piece in range(length // tap_count):
            window = intensity[:, piece * tap_count:piece * tap_count + 2 * tap_count]
            pieces.append(jnp.dot(window, table, preferred_element_type=jnp.float32))
        response = jnp.concatenate(pieces, 1).astype(jnp.bfloat16)
        for entry_index in range(entries):
            matrix = values_ref[slot_index, entry_index]
            mixed_real = jnp.dot(matrix, response[:square], preferred_element_type=jnp.float32).reshape(
                block_size, block_size, length
            )
            mixed_imag = jnp.dot(matrix, response[square:], preferred_element_type=jnp.float32).reshape(
                block_size, block_size, length
            )
            light = lights_ref[entries * slot_index + entry_index]
            light_real = fields_ref[0, light, :, tap_count:].astype(jnp.float32)[None]
            light_imag = fields_ref[1, light, :, tap_count:].astype(jnp.float32)[None]
            out_real = jnp.sum(light_real * mixed_real - light_imag * mixed_imag, axis=1)
            out_imag = jnp.sum(light_real * mixed_imag + light_imag * mixed_real, axis=1)
            target = targets_ref[entries * slot_index + entry_index]
            out_ref[target, 0] += out_real
            out_ref[target, 1] += out_imag
        return carry

    live = jnp.clip(live_ref[0], 0, slot_count)
    lax.fori_loop(0, live, body, 0)


def local(
    mode_fields, raman_taps, pair_blocks, light_blocks, target_blocks, raman_values, live_slots
):
    toeplitz = toeplitz_table(raman_taps)
    tap_count = toeplitz.shape[1]
    block_size = MB
    tm_count = lax.axis_size("tm")
    pair_count = lax.axis_size("pair")
    slot_count = pair_blocks.shape[1]
    entries = light_blocks.shape[2]
    mode_count = mode_fields.shape[1]
    blocks = mode_count // block_size
    live_count = live_slots[0]
    targets = target_blocks.reshape(slot_count, entries)
    halo = lax.ppermute(
        mode_fields[:, :, -tap_count:], "tm", [(k, k + 1) for k in range(tm_count - 1)]
    )
    window = jnp.concatenate([halo, mode_fields], 2)
    full_length = window.shape[2]
    length = full_length - tap_count
    fields = window.reshape(2, blocks, block_size, full_length)
    values = raman_values[0].reshape(slot_count, entries, block_size * block_size, block_size * block_size)
    smem = pl.BlockSpec(memory_space=pltpu.SMEM)
    vmem = pl.BlockSpec(memory_space=pltpu.VMEM)
    buffers = pl.pallas_call(
        slot_kernel,
        out_shape=jax.ShapeDtypeStruct((blocks, 2, block_size, length), jnp.float32),
        in_specs=[smem, smem, smem, smem, vmem, vmem, vmem],
        out_specs=vmem,
    )(
        pair_blocks[0].reshape(-1),
        light_blocks[0].reshape(-1),
        target_blocks.reshape(-1),
        live_slots,
        fields,
        toeplitz,
        values,
    )
    owned = blocks // pair_count
    received = lax.all_to_all(buffers, "pair", split_axis=0, concat_axis=0, tiled=True)
    shared = received.reshape(pair_count, owned, 2, block_size, length).sum(axis=0)
    result = jnp.transpose(shared, (1, 0, 2, 3)).reshape(2, owned * block_size, length)
    return result


def solution(mesh):
    return jax.shard_map(
        local,
        mesh=mesh,
        in_specs=(
            P(None, None, "tm"),
            P(),
            P("pair", None, None),
            P("pair", None, None),
            P("pair", None),
            P("pair", None, None, None),
            P("pair"),
        ),
        out_specs=P(None, "pair", "tm"),
        check_vma=False,
    )
```

```python
import jax
import jax.numpy as jnp
from jax import lax
from jax.sharding import PartitionSpec as P
from jax.experimental import pallas as pl
from jax.experimental.pallas import tpu as pltpu

MB = 8


def toeplitz_table(tap_values):
    tap_count = tap_values.shape[0]
    rows = 2 * tap_count
    period = rows + tap_count
    zeros = jnp.zeros((rows,), tap_values.dtype)
    base = jnp.concatenate([tap_values[tap_count - 1:], zeros, tap_values[: tap_count - 1]])
    tiled = jnp.tile(base, rows)[: rows * (period - 1)].reshape(rows, period - 1)
    return tiled[:, :tap_count]


def delayed(signal, toeplitz):
    tap_count = toeplitz.shape[1]
    out_length = signal.shape[1] - tap_count
    block_total = out_length // tap_count
    row_total = signal.shape[0]
    pieces = signal.reshape(row_total, block_total + 1, tap_count)
    windows = jnp.concatenate([pieces[:, :-1], pieces[:, 1:]], axis=2)
    flat_windows = windows.reshape(row_total * block_total, 2 * tap_count)
    result = jnp.dot(flat_windows, toeplitz, preferred_element_type=jnp.float32)
    return result.reshape(row_total, out_length)


def slot_partials(blocked, pair_ids, light_ids, values, toeplitz):
    tap_count = toeplitz.shape[1]
    block_size = blocked.shape[2]
    length = blocked.shape[3] - tap_count
    square = block_size * block_size
    left_field = blocked[pair_ids[0]]
    right_field = blocked[pair_ids[1]]
    left_real = left_field[0].astype(jnp.float32)[:, None]
    left_imag = left_field[1].astype(jnp.float32)[:, None]
    right_real = right_field[0].astype(jnp.float32)[None]
    right_imag = right_field[1].astype(jnp.float32)[None]
    real_part = (left_real * right_real + left_imag * right_imag).reshape(square, -1)
    imag_part = (left_imag * right_real - left_real * right_imag).reshape(square, -1)
    intensity = jnp.concatenate([real_part, imag_part], 0).astype(jnp.bfloat16)
    response = delayed(intensity, toeplitz).astype(jnp.bfloat16)
    partials = []
    for entry_index in range(values.shape[0]):
        matrix = values[entry_index].reshape(square, square)
        mixed_real = jnp.dot(matrix, response[:square], preferred_element_type=jnp.float32).reshape(
            block_size, block_size, length
        )
        mixed_imag = jnp.dot(matrix, response[square:], preferred_element_type=jnp.float32).reshape(
            block_size, block_size, length
        )
        light_field = blocked[light_ids[entry_index]][:, :, tap_count:]
        light_real = light_field[0][None]
        light_imag = light_field[1][None]
        out_real = jnp.sum(
            light_real.astype(jnp.float32) * mixed_real
            - light_imag.astype(jnp.float32) * mixed_imag,
            axis=1,
        )
        out_imag = jnp.sum(
            light_real.astype(jnp.float32) * mixed_imag
            + light_imag.astype(jnp.float32) * mixed_real,
            axis=1,
        )
        partials.append(jnp.stack([out_real, out_imag]))
    return partials


def slot_kernel(pairs_ref, lights_ref, targets_ref, live_ref, fields_ref, table_ref, values_ref, out_ref):
    block_size = fields_ref.shape[2]
    width = fields_ref.shape[3]
    length = out_ref.shape[3]
    tap_count = width - length
    square = block_size * block_size
    entries = values_ref.shape[1]
    slot_count = values_ref.shape[0]
    out_ref[...] = jnp.zeros(out_ref.shape, out_ref.dtype)
    table = table_ref[...]

    def body(slot_index, carry):
        left = pairs_ref[2 * slot_index]
        right = pairs_ref[2 * slot_index + 1]
        left_real = fields_ref[0, left].astype(jnp.float32)[:, None]
        left_imag = fields_ref[1, left].astype(jnp.float32)[:, None]
        right_real = fields_ref[0, right].astype(jnp.float32)[None]
        right_imag = fields_ref[1, right].astype(jnp.float32)[None]
        real_part = (left_real * right_real + left_imag * right_imag).reshape(square, width)
        imag_part = (left_imag * right_real - left_real * right_imag).reshape(square, width)
        intensity = jnp.concatenate([real_part, imag_part], 0).astype(jnp.bfloat16)
        pieces = []
        for piece in range(length // tap_count):
            window = intensity[:, piece * tap_count:piece * tap_count + 2 * tap_count]
            pieces.append(jnp.dot(window, table, preferred_element_type=jnp.float32))
        response = jnp.concatenate(pieces, 1).astype(jnp.bfloat16)
        for entry_index in range(entries):
            matrix = values_ref[slot_index, entry_index]
            mixed_real = jnp.dot(matrix, response[:square], preferred_element_type=jnp.float32).reshape(
                block_size, block_size, length
            )
            mixed_imag = jnp.dot(matrix, response[square:], preferred_element_type=jnp.float32).reshape(
                block_size, block_size, length
            )
            light = lights_ref[entries * slot_index + entry_index]
            light_real = fields_ref[0, light, :, tap_count:].astype(jnp.float32)[None]
            light_imag = fields_ref[1, light, :, tap_count:].astype(jnp.float32)[None]
            out_real = jnp.sum(light_real * mixed_real - light_imag * mixed_imag, axis=1)
            out_imag = jnp.sum(light_real * mixed_imag + light_imag * mixed_real, axis=1)
            target = targets_ref[entries * slot_index + entry_index]
            out_ref[target, 0] += out_real
            out_ref[target, 1] += out_imag
        return carry

    live = jnp.clip(live_ref[0], 0, slot_count)
    lax.fori_loop(0, live, body, 0)


def local(
    mode_fields, raman_taps, pair_blocks, light_blocks, target_blocks, raman_values, live_slots
):
    toeplitz = toeplitz_table(raman_taps)
    tap_count = toeplitz.shape[1]
    block_size = MB
    tm_count = lax.axis_size("tm")
    pair_count = lax.axis_size("pair")
    slot_count = pair_blocks.shape[1]
    entries = light_blocks.shape[2]
    mode_count = mode_fields.shape[1]
    blocks = mode_count // block_size
    halo = lax.ppermute(
        mode_fields[:, :, -tap_count:], "tm", [(k, k + 1) for k in range(tm_count - 1)]
    )
    window = jnp.concatenate([halo, mode_fields], 2)
    full_length = window.shape[2]
    length = full_length - tap_count
    fields = window.reshape(2, blocks, block_size, full_length)
    values = raman_values[0].reshape(slot_count, entries, block_size * block_size, block_size * block_size)
    smem = pl.BlockSpec(memory_space=pltpu.SMEM)
    vmem = pl.BlockSpec(memory_space=pltpu.VMEM)
    buffers = pl.pallas_call(
        slot_kernel,
        out_shape=jax.ShapeDtypeStruct((blocks, 2, block_size, length), jnp.float32),
        in_specs=[smem, smem, smem, smem, vmem, vmem, vmem],
        out_specs=vmem,
    )(
        pair_blocks[0].reshape(-1),
        light_blocks[0].reshape(-1),
        target_blocks.reshape(-1),
        live_slots,
        fields,
        toeplitz,
        values,
    )
    owned = blocks // pair_count
    shared = lax.psum_scatter(buffers, "pair", scatter_dimension=0, tiled=True)
    result = jnp.transpose(shared, (1, 0, 2, 3)).reshape(2, owned * block_size, length)
    return result


def solution(mesh):
    return jax.shard_map(
        local,
        mesh=mesh,
        in_specs=(
            P(None, None, "tm"),
            P(),
            P("pair", None, None),
            P("pair", None, None),
            P("pair", None),
            P("pair", None, None, None),
            P("pair"),
        ),
        out_specs=P(None, "pair", "tm"),
        check_vma=False,
    )
```

```python
import jax
import jax.numpy as jnp
from jax import lax
from jax.sharding import PartitionSpec as P
from jax.experimental import pallas as pl
from jax.experimental.pallas import tpu as pltpu

MB = 8


def toeplitz_table(tap_values):
    tap_count = tap_values.shape[0]
    rows = 2 * tap_count
    period = rows + tap_count
    zeros = jnp.zeros((rows,), tap_values.dtype)
    base = jnp.concatenate([tap_values[tap_count - 1:], zeros, tap_values[: tap_count - 1]])
    tiled = jnp.tile(base, rows)[: rows * (period - 1)].reshape(rows, period - 1)
    return tiled[:, :tap_count]


def delayed(signal, toeplitz):
    tap_count = toeplitz.shape[1]
    out_length = signal.shape[1] - tap_count
    block_total = out_length // tap_count
    row_total = signal.shape[0]
    pieces = signal.reshape(row_total, block_total + 1, tap_count)
    windows = jnp.concatenate([pieces[:, :-1], pieces[:, 1:]], axis=2)
    flat_windows = windows.reshape(row_total * block_total, 2 * tap_count)
    result = jnp.dot(flat_windows, toeplitz, preferred_element_type=jnp.float32)
    return result.reshape(row_total, out_length)


def slot_partials(blocked, pair_ids, light_ids, values, toeplitz):
    tap_count = toeplitz.shape[1]
    block_size = blocked.shape[2]
    length = blocked.shape[3] - tap_count
    square = block_size * block_size
    left_field = blocked[pair_ids[0]]
    right_field = blocked[pair_ids[1]]
    left_real = left_field[0].astype(jnp.float32)[:, None]
    left_imag = left_field[1].astype(jnp.float32)[:, None]
    right_real = right_field[0].astype(jnp.float32)[None]
    right_imag = right_field[1].astype(jnp.float32)[None]
    real_part = (left_real * right_real + left_imag * right_imag).reshape(square, -1)
    imag_part = (left_imag * right_real - left_real * right_imag).reshape(square, -1)
    intensity = jnp.concatenate([real_part, imag_part], 0).astype(jnp.bfloat16)
    response = delayed(intensity, toeplitz).astype(jnp.bfloat16)
    partials = []
    for entry_index in range(values.shape[0]):
        matrix = values[entry_index].reshape(square, square)
        mixed_real = jnp.dot(matrix, response[:square], preferred_element_type=jnp.float32).reshape(
            block_size, block_size, length
        )
        mixed_imag = jnp.dot(matrix, response[square:], preferred_element_type=jnp.float32).reshape(
            block_size, block_size, length
        )
        light_field = blocked[light_ids[entry_index]][:, :, tap_count:]
        light_real = light_field[0][None]
        light_imag = light_field[1][None]
        out_real = jnp.sum(
            light_real.astype(jnp.float32) * mixed_real
            - light_imag.astype(jnp.float32) * mixed_imag,
            axis=1,
        )
        out_imag = jnp.sum(
            light_real.astype(jnp.float32) * mixed_imag
            + light_imag.astype(jnp.float32) * mixed_real,
            axis=1,
        )
        partials.append(jnp.stack([out_real, out_imag]))
    return partials


def slot_kernel(pairs_ref, lights_ref, targets_ref, live_ref, fields_ref, table_ref, values_ref, out_ref):
    block_size = fields_ref.shape[2]
    width = fields_ref.shape[3]
    length = out_ref.shape[3]
    tap_count = width - length
    square = block_size * block_size
    entries = values_ref.shape[1]
    slot_count = values_ref.shape[0]
    out_ref[...] = jnp.zeros(out_ref.shape, out_ref.dtype)
    table = table_ref[...]

    def body(slot_index, carry):
        left = pairs_ref[2 * slot_index]
        right = pairs_ref[2 * slot_index + 1]
        left_real = fields_ref[0, left].astype(jnp.float32)[:, None]
        left_imag = fields_ref[1, left].astype(jnp.float32)[:, None]
        right_real = fields_ref[0, right].astype(jnp.float32)[None]
        right_imag = fields_ref[1, right].astype(jnp.float32)[None]
        real_part = (left_real * right_real + left_imag * right_imag).reshape(square, width)
        imag_part = (left_imag * right_real - left_real * right_imag).reshape(square, width)
        intensity = jnp.concatenate([real_part, imag_part], 0).astype(jnp.bfloat16)
        pieces = []
        for piece in range(length // tap_count):
            window = intensity[:, piece * tap_count:piece * tap_count + 2 * tap_count]
            pieces.append(jnp.dot(window, table, preferred_element_type=jnp.float32))
        response = jnp.concatenate(pieces, 1).astype(jnp.bfloat16)
        for entry_index in range(entries):
            matrix = values_ref[slot_index, entry_index]
            mixed_real = jnp.dot(matrix, response[:square], preferred_element_type=jnp.float32).reshape(
                block_size, block_size, length
            )
            mixed_imag = jnp.dot(matrix, response[square:], preferred_element_type=jnp.float32).reshape(
                block_size, block_size, length
            )
            light = lights_ref[entries * slot_index + entry_index]
            light_real = fields_ref[0, light, :, tap_count:].astype(jnp.float32)[None]
            light_imag = fields_ref[1, light, :, tap_count:].astype(jnp.float32)[None]
            out_real = jnp.sum(light_real * mixed_real - light_imag * mixed_imag, axis=1)
            out_imag = jnp.sum(light_real * mixed_imag + light_imag * mixed_real, axis=1)
            target = targets_ref[entries * slot_index + entry_index]
            out_ref[target, 0] += out_real
            out_ref[target, 1] += out_imag
        return carry

    live = jnp.clip(live_ref[0], 0, slot_count)
    lax.fori_loop(0, live, body, 0)


def exchange_kernel(buffers_ref, out_ref, recv_ref, send_sems, recv_sems):
    pair_count = buffers_ref.shape[0]
    me = lax.axis_index("pair")
    row = lax.axis_index("tm")
    mesh_ids = pl.DeviceIdType.MESH
    barrier = pltpu.get_barrier_semaphore()

    def greet(step, carry):
        peer = lax.rem(me + step, pair_count)
        pl.semaphore_signal(barrier, inc=1, device_id=(row, peer), device_id_type=mesh_ids)
        return carry

    lax.fori_loop(1, pair_count, greet, 0)
    pl.semaphore_wait(barrier, pair_count - 1)

    def outgoing(peer):
        return pltpu.make_async_remote_copy(
            src_ref=buffers_ref.at[peer],
            dst_ref=recv_ref.at[me],
            send_sem=send_sems.at[peer],
            recv_sem=recv_sems.at[me],
            device_id=(row, peer),
            device_id_type=mesh_ids,
        )

    def send(step, carry):
        outgoing(lax.rem(me + step, pair_count)).start()
        return carry

    lax.fori_loop(1, pair_count, send, 0)

    def gather(step, total):
        peer = lax.rem(me + pair_count - step, pair_count)
        incoming = pltpu.make_async_remote_copy(
            src_ref=buffers_ref.at[peer],
            dst_ref=recv_ref.at[peer],
            send_sem=send_sems.at[peer],
            recv_sem=recv_sems.at[peer],
            device_id=(row, peer),
            device_id_type=mesh_ids,
        )
        incoming.wait_recv()
        return total + recv_ref[peer]

    total = lax.fori_loop(1, pair_count, gather, buffers_ref[me])

    def finish(step, carry):
        outgoing(lax.rem(me + step, pair_count)).wait_send()
        return carry

    lax.fori_loop(1, pair_count, finish, 0)
    out_ref[...] = total


def local(
    mode_fields, raman_taps, pair_blocks, light_blocks, target_blocks, raman_values, live_slots
):
    toeplitz = toeplitz_table(raman_taps)
    tap_count = toeplitz.shape[1]
    block_size = MB
    tm_count = lax.axis_size("tm")
    pair_count = lax.axis_size("pair")
    slot_count = pair_blocks.shape[1]
    entries = light_blocks.shape[2]
    mode_count = mode_fields.shape[1]
    blocks = mode_count // block_size
    halo = lax.ppermute(
        mode_fields[:, :, -tap_count:], "tm", [(k, k + 1) for k in range(tm_count - 1)]
    )
    window = jnp.concatenate([halo, mode_fields], 2)
    full_length = window.shape[2]
    length = full_length - tap_count
    fields = window.reshape(2, blocks, block_size, full_length)
    values = raman_values[0].reshape(slot_count, entries, block_size * block_size, block_size * block_size)
    smem = pl.BlockSpec(memory_space=pltpu.SMEM)
    vmem = pl.BlockSpec(memory_space=pltpu.VMEM)
    buffers = pl.pallas_call(
        slot_kernel,
        out_shape=jax.ShapeDtypeStruct((blocks, 2, block_size, length), jnp.float32),
        in_specs=[smem, smem, smem, smem, vmem, vmem, vmem],
        out_specs=vmem,
    )(
        pair_blocks[0].reshape(-1),
        light_blocks[0].reshape(-1),
        target_blocks.reshape(-1),
        live_slots,
        fields,
        toeplitz,
        values,
    )
    owned = blocks // pair_count
    grouped = buffers.reshape(pair_count, owned, 2, block_size, length)
    shared = pl.pallas_call(
        exchange_kernel,
        out_shape=jax.ShapeDtypeStruct((owned, 2, block_size, length), jnp.float32),
        in_specs=[vmem],
        out_specs=vmem,
        scratch_shapes=[
            pltpu.VMEM(grouped.shape, jnp.float32),
            pltpu.SemaphoreType.DMA((pair_count,)),
            pltpu.SemaphoreType.DMA((pair_count,)),
        ],
        compiler_params=pltpu.CompilerParams(collective_id=0, has_side_effects=True),
    )(grouped)
    result = jnp.transpose(shared, (1, 0, 2, 3)).reshape(2, owned * block_size, length)
    return result


def solution(mesh):
    return jax.shard_map(
        local,
        mesh=mesh,
        in_specs=(
            P(None, None, "tm"),
            P(),
            P("pair", None, None),
            P("pair", None, None),
            P("pair", None),
            P("pair", None, None, None),
            P("pair"),
        ),
        out_specs=P(None, "pair", "tm"),
        check_vma=False,
    )
```

```python
import jax
import jax.numpy as jnp
from jax import lax
from jax.sharding import PartitionSpec as P
from jax.experimental import pallas as pl
from jax.experimental.pallas import tpu as pltpu

MB = 8


def toeplitz_table(tap_values):
    tap_count = tap_values.shape[0]
    rows = 2 * tap_count
    period = rows + tap_count
    zeros = jnp.zeros((rows,), tap_values.dtype)
    base = jnp.concatenate([tap_values[tap_count - 1:], zeros, tap_values[: tap_count - 1]])
    tiled = jnp.tile(base, rows)[: rows * (period - 1)].reshape(rows, period - 1)
    return tiled[:, :tap_count]


def delayed(signal, toeplitz):
    tap_count = toeplitz.shape[1]
    out_length = signal.shape[1] - tap_count
    block_total = out_length // tap_count
    row_total = signal.shape[0]
    pieces = signal.reshape(row_total, block_total + 1, tap_count)
    windows = jnp.concatenate([pieces[:, :-1], pieces[:, 1:]], axis=2)
    flat_windows = windows.reshape(row_total * block_total, 2 * tap_count)
    result = jnp.dot(flat_windows, toeplitz, preferred_element_type=jnp.float32)
    return result.reshape(row_total, out_length)


def slot_partials(blocked, pair_ids, light_ids, values, toeplitz):
    tap_count = toeplitz.shape[1]
    block_size = blocked.shape[2]
    length = blocked.shape[3] - tap_count
    square = block_size * block_size
    left_field = blocked[pair_ids[0]]
    right_field = blocked[pair_ids[1]]
    left_real = left_field[0].astype(jnp.float32)[:, None]
    left_imag = left_field[1].astype(jnp.float32)[:, None]
    right_real = right_field[0].astype(jnp.float32)[None]
    right_imag = right_field[1].astype(jnp.float32)[None]
    real_part = (left_real * right_real + left_imag * right_imag).reshape(square, -1)
    imag_part = (left_imag * right_real - left_real * right_imag).reshape(square, -1)
    intensity = jnp.concatenate([real_part, imag_part], 0).astype(jnp.bfloat16)
    response = delayed(intensity, toeplitz).astype(jnp.bfloat16)
    partials = []
    for entry_index in range(values.shape[0]):
        matrix = values[entry_index].reshape(square, square)
        mixed_real = jnp.dot(matrix, response[:square], preferred_element_type=jnp.float32).reshape(
            block_size, block_size, length
        )
        mixed_imag = jnp.dot(matrix, response[square:], preferred_element_type=jnp.float32).reshape(
            block_size, block_size, length
        )
        light_field = blocked[light_ids[entry_index]][:, :, tap_count:]
        light_real = light_field[0][None]
        light_imag = light_field[1][None]
        out_real = jnp.sum(
            light_real.astype(jnp.float32) * mixed_real
            - light_imag.astype(jnp.float32) * mixed_imag,
            axis=1,
        )
        out_imag = jnp.sum(
            light_real.astype(jnp.float32) * mixed_imag
            + light_imag.astype(jnp.float32) * mixed_real,
            axis=1,
        )
        partials.append(jnp.stack([out_real, out_imag]))
    return partials


def slot_kernel(pairs_ref, lights_ref, targets_ref, live_ref, fields_ref, table_ref, values_ref, out_ref, acc_ref):
    block_size = fields_ref.shape[2]
    width = fields_ref.shape[3]
    length = out_ref.shape[3]
    tap_count = width - length
    square = block_size * block_size
    entries = values_ref.shape[1]
    slot_count = values_ref.shape[0]
    acc_ref[...] = jnp.zeros(acc_ref.shape, acc_ref.dtype)
    table = table_ref[...]

    def body(slot_index, carry):
        left = pairs_ref[2 * slot_index]
        right = pairs_ref[2 * slot_index + 1]
        left_real = fields_ref[0, left].astype(jnp.float32)[:, None]
        left_imag = fields_ref[1, left].astype(jnp.float32)[:, None]
        right_real = fields_ref[0, right].astype(jnp.float32)[None]
        right_imag = fields_ref[1, right].astype(jnp.float32)[None]
        real_part = (left_real * right_real + left_imag * right_imag).reshape(square, width)
        imag_part = (left_imag * right_real - left_real * right_imag).reshape(square, width)
        intensity = jnp.concatenate([real_part, imag_part], 0).astype(jnp.bfloat16)
        pieces = []
        for piece in range(length // tap_count):
            window = intensity[:, piece * tap_count:piece * tap_count + 2 * tap_count]
            pieces.append(jnp.dot(window, table, preferred_element_type=jnp.float32))
        response = jnp.concatenate(pieces, 1).astype(jnp.bfloat16)
        for entry_index in range(entries):
            matrix = values_ref[slot_index, entry_index]
            mixed_real = jnp.dot(matrix, response[:square], preferred_element_type=jnp.float32).reshape(
                block_size, block_size, length
            )
            mixed_imag = jnp.dot(matrix, response[square:], preferred_element_type=jnp.float32).reshape(
                block_size, block_size, length
            )
            light = lights_ref[entries * slot_index + entry_index]
            light_real = fields_ref[0, light, :, tap_count:].astype(jnp.float32)[None]
            light_imag = fields_ref[1, light, :, tap_count:].astype(jnp.float32)[None]
            out_real = jnp.sum(light_real * mixed_real - light_imag * mixed_imag, axis=1)
            out_imag = jnp.sum(light_real * mixed_imag + light_imag * mixed_real, axis=1)
            target = targets_ref[entries * slot_index + entry_index]
            acc_ref[target, 0] += out_real
            acc_ref[target, 1] += out_imag
        return carry

    live = jnp.clip(live_ref[0], 0, slot_count)
    lax.fori_loop(0, live, body, 0)
    out_ref[...] = acc_ref[...].astype(out_ref.dtype)


def exchange_kernel(buffers_ref, out_ref, recv_ref, send_sems, recv_sems):
    pair_count = buffers_ref.shape[0]
    me = lax.axis_index("pair")
    row = lax.axis_index("tm")
    mesh_ids = pl.DeviceIdType.MESH
    barrier = pltpu.get_barrier_semaphore()

    def greet(step, carry):
        peer = lax.rem(me + step, pair_count)
        pl.semaphore_signal(barrier, inc=1, device_id=(row, peer), device_id_type=mesh_ids)
        return carry

    lax.fori_loop(1, pair_count, greet, 0)
    pl.semaphore_wait(barrier, pair_count - 1)

    def outgoing(peer):
        return pltpu.make_async_remote_copy(
            src_ref=buffers_ref.at[peer],
            dst_ref=recv_ref.at[me],
            send_sem=send_sems.at[peer],
            recv_sem=recv_sems.at[me],
            device_id=(row, peer),
            device_id_type=mesh_ids,
        )

    def send(step, carry):
        outgoing(lax.rem(me + step, pair_count)).start()
        return carry

    lax.fori_loop(1, pair_count, send, 0)

    def gather(step, total):
        peer = lax.rem(me + pair_count - step, pair_count)
        incoming = pltpu.make_async_remote_copy(
            src_ref=buffers_ref.at[peer],
            dst_ref=recv_ref.at[peer],
            send_sem=send_sems.at[peer],
            recv_sem=recv_sems.at[peer],
            device_id=(row, peer),
            device_id_type=mesh_ids,
        )
        incoming.wait_recv()
        return total + recv_ref[peer].astype(jnp.float32)

    total = lax.fori_loop(1, pair_count, gather, buffers_ref[me].astype(jnp.float32))

    def finish(step, carry):
        outgoing(lax.rem(me + step, pair_count)).wait_send()
        return carry

    lax.fori_loop(1, pair_count, finish, 0)
    out_ref[...] = total


def local(
    mode_fields, raman_taps, pair_blocks, light_blocks, target_blocks, raman_values, live_slots
):
    toeplitz = toeplitz_table(raman_taps)
    tap_count = toeplitz.shape[1]
    block_size = MB
    tm_count = lax.axis_size("tm")
    pair_count = lax.axis_size("pair")
    slot_count = pair_blocks.shape[1]
    entries = light_blocks.shape[2]
    mode_count = mode_fields.shape[1]
    blocks = mode_count // block_size
    halo = lax.ppermute(
        mode_fields[:, :, -tap_count:], "tm", [(k, k + 1) for k in range(tm_count - 1)]
    )
    window = jnp.concatenate([halo, mode_fields], 2)
    full_length = window.shape[2]
    length = full_length - tap_count
    fields = window.reshape(2, blocks, block_size, full_length)
    values = raman_values[0].reshape(slot_count, entries, block_size * block_size, block_size * block_size)
    smem = pl.BlockSpec(memory_space=pltpu.SMEM)
    vmem = pl.BlockSpec(memory_space=pltpu.VMEM)
    buffers = pl.pallas_call(
        slot_kernel,
        out_shape=jax.ShapeDtypeStruct((blocks, 2, block_size, length), jnp.bfloat16),
        in_specs=[smem, smem, smem, smem, vmem, vmem, vmem],
        out_specs=vmem,
        scratch_shapes=[pltpu.VMEM((blocks, 2, block_size, length), jnp.float32)],
    )(
        pair_blocks[0].reshape(-1),
        light_blocks[0].reshape(-1),
        target_blocks.reshape(-1),
        live_slots,
        fields,
        toeplitz,
        values,
    )
    owned = blocks // pair_count
    grouped = buffers.reshape(pair_count, owned, 2, block_size, length)
    shared = pl.pallas_call(
        exchange_kernel,
        out_shape=jax.ShapeDtypeStruct((owned, 2, block_size, length), jnp.float32),
        in_specs=[vmem],
        out_specs=vmem,
        scratch_shapes=[
            pltpu.VMEM(grouped.shape, grouped.dtype),
            pltpu.SemaphoreType.DMA((pair_count,)),
            pltpu.SemaphoreType.DMA((pair_count,)),
        ],
        compiler_params=pltpu.CompilerParams(collective_id=0, has_side_effects=True),
    )(grouped)
    result = jnp.transpose(shared, (1, 0, 2, 3)).reshape(2, owned * block_size, length)
    return result


def solution(mesh):
    return jax.shard_map(
        local,
        mesh=mesh,
        in_specs=(
            P(None, None, "tm"),
            P(),
            P("pair", None, None),
            P("pair", None, None),
            P("pair", None),
            P("pair", None, None, None),
            P("pair"),
        ),
        out_specs=P(None, "pair", "tm"),
        check_vma=False,
    )
```

```python
import functools

import jax
import jax.numpy as jnp
from jax import lax
from jax.sharding import PartitionSpec as P
from jax.experimental import pallas as pl
from jax.experimental.pallas import tpu as pltpu

MB = 8


def toeplitz_table(tap_values):
    tap_count = tap_values.shape[0]
    rows = 2 * tap_count
    period = rows + tap_count
    zeros = jnp.zeros((rows,), tap_values.dtype)
    base = jnp.concatenate([tap_values[tap_count - 1:], zeros, tap_values[: tap_count - 1]])
    tiled = jnp.tile(base, rows)[: rows * (period - 1)].reshape(rows, period - 1)
    return tiled[:, :tap_count]


def fused_kernel(
    slot_count, entries,
    ints_ref, halo_ref, fields_ref, table_ref, values_ref, out_ref,
    partials_ref, send_ref, recv_ref, send_sems, recv_sems,
):
    block_size = fields_ref.shape[2]
    length = fields_ref.shape[3]
    tap_count = halo_ref.shape[3]
    width = length + tap_count
    square = block_size * block_size
    pair_count = send_ref.shape[0]
    owned = send_ref.shape[1]
    light_base = 2 * slot_count
    pick_base = light_base + entries * slot_count
    zero_row = slot_count * entries
    me = lax.axis_index("pair")
    row = lax.axis_index("tm")
    mesh_ids = pl.DeviceIdType.MESH
    barrier = pltpu.get_barrier_semaphore()

    def greet(step, carry):
        peer = lax.rem(me + step, pair_count)
        pl.semaphore_signal(barrier, inc=1, device_id=(row, peer), device_id_type=mesh_ids)
        return carry

    lax.fori_loop(1, pair_count, greet, 0)

    partials_ref[zero_row] = jnp.zeros(partials_ref.shape[1:], partials_ref.dtype)
    table = table_ref[...]

    def window(part, block):
        return jnp.concatenate([halo_ref[part, block], fields_ref[part, block]], 1).astype(jnp.float32)

    def body(slot_index, carry):
        left = ints_ref[2 * slot_index]
        right = ints_ref[2 * slot_index + 1]
        left_real = window(0, left)[:, None]
        left_imag = window(1, left)[:, None]
        right_real = window(0, right)[None]
        right_imag = window(1, right)[None]
        real_part = (left_real * right_real + left_imag * right_imag).reshape(square, width)
        imag_part = (left_imag * right_real - left_real * right_imag).reshape(square, width)
        intensity = jnp.concatenate([real_part, imag_part], 0).astype(jnp.bfloat16)
        pieces = []
        for piece in range(length // tap_count):
            span = intensity[:, piece * tap_count:piece * tap_count + 2 * tap_count]
            pieces.append(jnp.dot(span, table, preferred_element_type=jnp.float32))
        response = jnp.concatenate(pieces, 1).astype(jnp.bfloat16)
        for entry_index in range(entries):
            matrix = values_ref[slot_index, entry_index]
            mixed_real = jnp.dot(matrix, response[:square], preferred_element_type=jnp.float32).reshape(
                block_size, block_size, length
            )
            mixed_imag = jnp.dot(matrix, response[square:], preferred_element_type=jnp.float32).reshape(
                block_size, block_size, length
            )
            light = ints_ref[light_base + entries * slot_index + entry_index]
            light_real = fields_ref[0, light].astype(jnp.float32)[None]
            light_imag = fields_ref[1, light].astype(jnp.float32)[None]
            out_real = jnp.sum(light_real * mixed_real - light_imag * mixed_imag, axis=1)
            out_imag = jnp.sum(light_real * mixed_imag + light_imag * mixed_real, axis=1)
            partials_ref[entries * slot_index + entry_index, 0] = out_real
            partials_ref[entries * slot_index + entry_index, 1] = out_imag
        return carry

    lax.fori_loop(0, slot_count, body, 0)

    def block_sum(peer, part):
        block = peer * owned + part
        first = ints_ref[pick_base + 2 * block]
        second = ints_ref[pick_base + 2 * block + 1]
        return partials_ref[first] + partials_ref[second]

    pl.semaphore_wait(barrier, pair_count - 1)

    def outgoing(peer):
        return pltpu.make_async_remote_copy(
            src_ref=send_ref.at[peer],
            dst_ref=recv_ref.at[me],
            send_sem=send_sems.at[peer],
            recv_sem=recv_sems.at[me],
            device_id=(row, peer),
            device_id_type=mesh_ids,
        )

    def send(step, carry):
        peer = lax.rem(me + step, pair_count)
        for part in range(owned):
            send_ref[peer, part] = block_sum(peer, part).astype(send_ref.dtype)
        outgoing(peer).start()
        return carry

    lax.fori_loop(1, pair_count, send, 0)

    def gather(step, total):
        peer = lax.rem(me + pair_count - step, pair_count)
        incoming = pltpu.make_async_remote_copy(
            src_ref=send_ref.at[peer],
            dst_ref=recv_ref.at[peer],
            send_sem=send_sems.at[peer],
            recv_sem=recv_sems.at[peer],
            device_id=(row, peer),
            device_id_type=mesh_ids,
        )
        incoming.wait_recv()
        return total + recv_ref[peer].astype(jnp.float32)

    own = jnp.stack([block_sum(me, part) for part in range(owned)])
    total = lax.fori_loop(1, pair_count, gather, own)

    def finish(step, carry):
        outgoing(lax.rem(me + step, pair_count)).wait_send()
        return carry

    lax.fori_loop(1, pair_count, finish, 0)
    out_ref[...] = total


def local(
    mode_fields, raman_taps, pair_blocks, light_blocks, target_blocks, raman_values, live_slots
):
    toeplitz = toeplitz_table(raman_taps)
    tap_count = toeplitz.shape[1]
    block_size = MB
    tm_count = lax.axis_size("tm")
    pair_count = lax.axis_size("pair")
    slot_count = pair_blocks.shape[1]
    entries = light_blocks.shape[2]
    mode_count = mode_fields.shape[1]
    length = mode_fields.shape[2]
    blocks = mode_count // block_size
    owned = blocks // pair_count
    rows = slot_count * entries
    halo = lax.ppermute(
        mode_fields[:, :, -tap_count:], "tm", [(k, k + 1) for k in range(tm_count - 1)]
    )
    halo = halo.reshape(2, blocks, block_size, tap_count)
    fields = mode_fields.reshape(2, blocks, block_size, length)
    square = block_size * block_size
    values = raman_values[0].reshape(slot_count, entries, square, square)
    row_index = jnp.arange(rows, dtype=jnp.int32)
    live_rows = row_index // entries < live_slots[0]
    feeds = (target_blocks.reshape(1, rows) == jnp.arange(blocks, dtype=jnp.int32)[:, None]) & live_rows[None]
    count = jnp.sum(feeds.astype(jnp.int32), axis=1)
    first = jnp.where(count >= 1, jnp.argmax(feeds, axis=1).astype(jnp.int32), rows)
    last = rows - 1 - jnp.argmax(feeds[:, ::-1], axis=1).astype(jnp.int32)
    second = jnp.where(count >= 2, last, rows)
    ints = jnp.concatenate(
        [pair_blocks.reshape(-1), light_blocks.reshape(-1), jnp.stack([first, second], 1).reshape(-1)]
    )
    smem = pl.BlockSpec(memory_space=pltpu.SMEM)
    vmem = pl.BlockSpec(memory_space=pltpu.VMEM)
    exchange_shape = (pair_count, owned, 2, block_size, length)
    shared = pl.pallas_call(
        functools.partial(fused_kernel, slot_count, entries),
        out_shape=jax.ShapeDtypeStruct((owned, 2, block_size, length), jnp.float32),
        in_specs=[smem, vmem, vmem, vmem, vmem],
        out_specs=vmem,
        scratch_shapes=[
            pltpu.VMEM((rows + 1, 2, block_size, length), jnp.float32),
            pltpu.VMEM(exchange_shape, jnp.bfloat16),
            pltpu.VMEM(exchange_shape, jnp.bfloat16),
            pltpu.SemaphoreType.DMA((pair_count,)),
            pltpu.SemaphoreType.DMA((pair_count,)),
        ],
        compiler_params=pltpu.CompilerParams(collective_id=0, has_side_effects=True),
    )(ints, halo, fields, toeplitz, values)
    result = jnp.transpose(shared, (1, 0, 2, 3)).reshape(2, owned * block_size, length)
    return result


def solution(mesh):
    return jax.shard_map(
        local,
        mesh=mesh,
        in_specs=(
            P(None, None, "tm"),
            P(),
            P("pair", None, None),
            P("pair", None, None),
            P("pair", None),
            P("pair", None, None, None),
            P("pair"),
        ),
        out_specs=P(None, "pair", "tm"),
        check_vma=False,
    )
```

```python
import functools

import jax
import jax.numpy as jnp
from jax import lax
from jax.sharding import PartitionSpec as P
from jax.experimental import pallas as pl
from jax.experimental.pallas import tpu as pltpu

MB = 8
Y_IN_PAIR = 4


def toeplitz_table(tap_values):
    tap_count = tap_values.shape[0]
    rows = 2 * tap_count
    period = rows + tap_count
    zeros = jnp.zeros((rows,), tap_values.dtype)
    base = jnp.concatenate([tap_values[tap_count - 1:], zeros, tap_values[: tap_count - 1]])
    tiled = jnp.tile(base, rows)[: rows * (period - 1)].reshape(rows, period - 1)
    return tiled[:, :tap_count]


def fused_kernel(
    slot_count, entries,
    ints_ref, halo_ref, fields_ref, table_ref, values_ref, out_ref,
    partials_ref, send_ref, recv_ref, stage_ref, final_ref,
    send_sems, recv_sems, stage_send_sems, stage_recv_sems,
):
    block_size = fields_ref.shape[2]
    length = fields_ref.shape[3]
    tap_count = halo_ref.shape[3]
    width = length + tap_count
    square = block_size * block_size
    owned = send_ref.shape[2]
    light_base = 2 * slot_count
    pick_base = light_base + entries * slot_count
    zero_row = slot_count * entries
    me = lax.axis_index("pair")
    row = lax.axis_index("tm")
    mesh_ids = pl.DeviceIdType.MESH
    barrier = pltpu.get_barrier_semaphore()

    y_count = send_ref.shape[0]
    z_count = stage_ref.shape[0]

    def greet_y(step, carry):
        peer = (me // y_count) * y_count + lax.rem(lax.rem(me, y_count) + step, y_count)
        pl.semaphore_signal(barrier, inc=1, device_id=(row, peer), device_id_type=mesh_ids)
        return carry

    def greet_z(step, carry):
        peer = lax.rem(me // y_count + step, z_count) * y_count + lax.rem(me, y_count)
        pl.semaphore_signal(barrier, inc=1, device_id=(row, peer), device_id_type=mesh_ids)
        return carry

    lax.fori_loop(1, y_count, greet_y, 0)
    lax.fori_loop(1, z_count, greet_z, 0)

    partials_ref[zero_row] = jnp.zeros(partials_ref.shape[1:], partials_ref.dtype)
    table = table_ref[...]

    def window(part, block):
        return jnp.concatenate([halo_ref[part, block], fields_ref[part, block]], 1).astype(jnp.float32)

    def body(slot_index, carry):
        left = ints_ref[2 * slot_index]
        right = ints_ref[2 * slot_index + 1]
        left_real = window(0, left)[:, None]
        left_imag = window(1, left)[:, None]
        right_real = window(0, right)[None]
        right_imag = window(1, right)[None]
        real_part = (left_real * right_real + left_imag * right_imag).reshape(square, width)
        imag_part = (left_imag * right_real - left_real * right_imag).reshape(square, width)
        intensity = jnp.concatenate([real_part, imag_part], 0).astype(jnp.bfloat16)
        pieces = []
        for piece in range(length // tap_count):
            span = intensity[:, piece * tap_count:piece * tap_count + 2 * tap_count]
            pieces.append(jnp.dot(span, table, preferred_element_type=jnp.float32))
        response = jnp.concatenate(pieces, 1).astype(jnp.bfloat16)
        for entry_index in range(entries):
            matrix = values_ref[slot_index, entry_index]
            mixed_real = jnp.dot(matrix, response[:square], preferred_element_type=jnp.float32).reshape(
                block_size, block_size, length
            )
            mixed_imag = jnp.dot(matrix, response[square:], preferred_element_type=jnp.float32).reshape(
                block_size, block_size, length
            )
            light = ints_ref[light_base + entries * slot_index + entry_index]
            light_real = fields_ref[0, light].astype(jnp.float32)[None]
            light_imag = fields_ref[1, light].astype(jnp.float32)[None]
            out_real = jnp.sum(light_real * mixed_real - light_imag * mixed_imag, axis=1)
            out_imag = jnp.sum(light_real * mixed_imag + light_imag * mixed_real, axis=1)
            partials_ref[entries * slot_index + entry_index, 0] = out_real
            partials_ref[entries * slot_index + entry_index, 1] = out_imag
        return carry

    lax.fori_loop(0, slot_count, body, 0)

    def block_sum(peer, part):
        block = peer * owned + part
        first = ints_ref[pick_base + 2 * block]
        second = ints_ref[pick_base + 2 * block + 1]
        return partials_ref[first] + partials_ref[second]

    group = send_ref.shape[0]
    rings = stage_ref.shape[0]
    my_y = lax.rem(me, group)
    my_z = me // group
    pl.semaphore_wait(barrier, group - 1 + rings - 1)

    def outgoing_y(peer_y):
        return pltpu.make_async_remote_copy(
            src_ref=send_ref.at[peer_y],
            dst_ref=recv_ref.at[my_y],
            send_sem=send_sems.at[peer_y],
            recv_sem=recv_sems.at[my_y],
            device_id=(row, my_z * group + peer_y),
            device_id_type=mesh_ids,
        )

    def send_y(step, carry):
        peer_y = lax.rem(my_y + step, group)
        for ring in range(rings):
            for part in range(owned):
                send_ref[peer_y, ring, part] = block_sum(ring * group + peer_y, part).astype(send_ref.dtype)
        outgoing_y(peer_y).start()
        return carry

    lax.fori_loop(1, group, send_y, 0)
    for ring in range(rings):
        for part in range(owned):
            stage_ref[ring, part] = block_sum(ring * group + my_y, part)

    def gather_y(step, carry):
        peer_y = lax.rem(my_y + group - step, group)
        incoming = pltpu.make_async_remote_copy(
            src_ref=send_ref.at[peer_y],
            dst_ref=recv_ref.at[peer_y],
            send_sem=send_sems.at[peer_y],
            recv_sem=recv_sems.at[peer_y],
            device_id=(row, my_z * group + peer_y),
            device_id_type=mesh_ids,
        )
        incoming.wait_recv()
        stage_ref[...] += recv_ref[peer_y].astype(jnp.float32)
        return carry

    lax.fori_loop(1, group, gather_y, 0)

    def outgoing_z(peer_z):
        return pltpu.make_async_remote_copy(
            src_ref=stage_ref.at[peer_z],
            dst_ref=final_ref.at[my_z],
            send_sem=stage_send_sems.at[peer_z],
            recv_sem=stage_recv_sems.at[my_z],
            device_id=(row, peer_z * group + my_y),
            device_id_type=mesh_ids,
        )

    def send_z(step, carry):
        outgoing_z(lax.rem(my_z + step, rings)).start()
        return carry

    lax.fori_loop(1, rings, send_z, 0)

    def gather_z(step, total):
        peer_z = lax.rem(my_z + rings - step, rings)
        incoming = pltpu.make_async_remote_copy(
            src_ref=stage_ref.at[peer_z],
            dst_ref=final_ref.at[peer_z],
            send_sem=stage_send_sems.at[peer_z],
            recv_sem=stage_recv_sems.at[peer_z],
            device_id=(row, peer_z * group + my_y),
            device_id_type=mesh_ids,
        )
        incoming.wait_recv()
        return total + final_ref[peer_z]

    total = lax.fori_loop(1, rings, gather_z, stage_ref[my_z])

    def finish_y(step, carry):
        outgoing_y(lax.rem(my_y + step, group)).wait_send()
        return carry

    def finish_z(step, carry):
        outgoing_z(lax.rem(my_z + step, rings)).wait_send()
        return carry

    lax.fori_loop(1, group, finish_y, 0)
    lax.fori_loop(1, rings, finish_z, 0)
    out_ref[...] = total


def local(
    mode_fields, raman_taps, pair_blocks, light_blocks, target_blocks, raman_values, live_slots
):
    toeplitz = toeplitz_table(raman_taps)
    tap_count = toeplitz.shape[1]
    block_size = MB
    tm_count = lax.axis_size("tm")
    pair_count = lax.axis_size("pair")
    slot_count = pair_blocks.shape[1]
    entries = light_blocks.shape[2]
    mode_count = mode_fields.shape[1]
    length = mode_fields.shape[2]
    blocks = mode_count // block_size
    owned = blocks // pair_count
    rows = slot_count * entries
    halo = lax.ppermute(
        mode_fields[:, :, -tap_count:], "tm", [(k, k + 1) for k in range(tm_count - 1)]
    )
    halo = halo.reshape(2, blocks, block_size, tap_count)
    fields = mode_fields.reshape(2, blocks, block_size, length)
    square = block_size * block_size
    values = raman_values[0].reshape(slot_count, entries, square, square)
    row_index = jnp.arange(rows, dtype=jnp.int32)
    live_rows = row_index // entries < live_slots[0]
    feeds = (target_blocks.reshape(1, rows) == jnp.arange(blocks, dtype=jnp.int32)[:, None]) & live_rows[None]
    first = jnp.min(jnp.where(feeds, row_index[None], rows), axis=1)
    last = jnp.max(jnp.where(feeds, row_index[None], -1), axis=1)
    second = jnp.where(last > first, last, rows)
    ints = jnp.concatenate(
        [pair_blocks.reshape(-1), light_blocks.reshape(-1), jnp.stack([first, second], 1).reshape(-1)]
    )
    smem = pl.BlockSpec(memory_space=pltpu.SMEM)
    vmem = pl.BlockSpec(memory_space=pltpu.VMEM)
    z_count = pair_count // Y_IN_PAIR
    exchange_shape = (Y_IN_PAIR, z_count, owned, 2, block_size, length)
    stage_shape = (z_count, owned, 2, block_size, length)
    shared = pl.pallas_call(
        functools.partial(fused_kernel, slot_count, entries),
        out_shape=jax.ShapeDtypeStruct((owned, 2, block_size, length), jnp.float32),
        in_specs=[smem, vmem, vmem, vmem, vmem],
        out_specs=vmem,
        scratch_shapes=[
            pltpu.VMEM((rows + 1, 2, block_size, length), jnp.float32),
            pltpu.VMEM(exchange_shape, jnp.bfloat16),
            pltpu.VMEM(exchange_shape, jnp.bfloat16),
            pltpu.VMEM(stage_shape, jnp.float32),
            pltpu.VMEM(stage_shape, jnp.float32),
            pltpu.SemaphoreType.DMA((Y_IN_PAIR,)),
            pltpu.SemaphoreType.DMA((Y_IN_PAIR,)),
            pltpu.SemaphoreType.DMA((z_count,)),
            pltpu.SemaphoreType.DMA((z_count,)),
        ],
        compiler_params=pltpu.CompilerParams(collective_id=0, has_side_effects=True),
    )(ints, halo, fields, toeplitz, values)
    result = jnp.transpose(shared, (1, 0, 2, 3)).reshape(2, owned * block_size, length)
    return result


def solution(mesh):
    return jax.shard_map(
        local,
        mesh=mesh,
        in_specs=(
            P(None, None, "tm"),
            P(),
            P("pair", None, None),
            P("pair", None, None),
            P("pair", None),
            P("pair", None, None, None),
            P("pair"),
        ),
        out_specs=P(None, "pair", "tm"),
        check_vma=False,
    )
```

```python
import functools

import jax
import jax.numpy as jnp
from jax import lax
from jax.sharding import PartitionSpec as P
from jax.experimental import pallas as pl
from jax.experimental.pallas import tpu as pltpu

MB = 8


def toeplitz_table(tap_values):
    tap_count = tap_values.shape[0]
    rows = 2 * tap_count
    period = rows + tap_count
    zeros = jnp.zeros((rows,), tap_values.dtype)
    base = jnp.concatenate([tap_values[tap_count - 1:], zeros, tap_values[: tap_count - 1]])
    tiled = jnp.tile(base, rows)[: rows * (period - 1)].reshape(rows, period - 1)
    return tiled[:, :tap_count]


def fused_kernel(
    slot_count, entries,
    ints_ref, halo_ref, fields_ref, table_ref, values_ref, out_ref,
    partials_ref, send_ref, recv_ref, send_sems, recv_sems,
):
    block_size = fields_ref.shape[2]
    length = fields_ref.shape[3]
    tap_count = halo_ref.shape[3]
    width = length + tap_count
    square = block_size * block_size
    pair_count = send_ref.shape[0]
    owned = send_ref.shape[1]
    light_base = 2 * slot_count
    pick_base = light_base + entries * slot_count
    zero_row = slot_count * entries
    me = lax.axis_index("pair")
    row = lax.axis_index("tm")
    mesh_ids = pl.DeviceIdType.MESH
    barrier = pltpu.get_barrier_semaphore()

    def greet(step, carry):
        peer = lax.rem(me + step, pair_count)
        pl.semaphore_signal(barrier, inc=1, device_id=(row, peer), device_id_type=mesh_ids)
        return carry

    lax.fori_loop(1, pair_count, greet, 0)

    partials_ref[zero_row] = jnp.zeros(partials_ref.shape[1:], partials_ref.dtype)
    table = table_ref[...]

    def window(part, block):
        return jnp.concatenate([halo_ref[part, block], fields_ref[part, block]], 1).astype(jnp.float32)

    def body(slot_index, carry):
        left = ints_ref[2 * slot_index]
        right = ints_ref[2 * slot_index + 1]
        left_real = window(0, left)[:, None]
        left_imag = window(1, left)[:, None]
        right_real = window(0, right)[None]
        right_imag = window(1, right)[None]
        real_part = (left_real * right_real + left_imag * right_imag).reshape(square, width)
        imag_part = (left_imag * right_real - left_real * right_imag).reshape(square, width)
        intensity = jnp.concatenate([real_part, imag_part], 0).astype(jnp.bfloat16)
        pieces = []
        for piece in range(length // tap_count):
            span = intensity[:, piece * tap_count:piece * tap_count + 2 * tap_count]
            pieces.append(jnp.dot(span, table, preferred_element_type=jnp.float32))
        response = jnp.concatenate(pieces, 1).astype(jnp.bfloat16)
        for entry_index in range(entries):
            matrix = values_ref[slot_index, entry_index]
            mixed_real = jnp.dot(matrix, response[:square], preferred_element_type=jnp.float32).reshape(
                block_size, block_size, length
            )
            mixed_imag = jnp.dot(matrix, response[square:], preferred_element_type=jnp.float32).reshape(
                block_size, block_size, length
            )
            light = ints_ref[light_base + entries * slot_index + entry_index]
            light_real = fields_ref[0, light].astype(jnp.float32)[None]
            light_imag = fields_ref[1, light].astype(jnp.float32)[None]
            out_real = jnp.sum(light_real * mixed_real - light_imag * mixed_imag, axis=1)
            out_imag = jnp.sum(light_real * mixed_imag + light_imag * mixed_real, axis=1)
            partials_ref[entries * slot_index + entry_index, 0] = out_real
            partials_ref[entries * slot_index + entry_index, 1] = out_imag
        return carry

    lax.fori_loop(0, slot_count, body, 0)

    def block_sum(peer, part):
        block = peer * owned + part
        first = ints_ref[pick_base + 2 * block]
        second = ints_ref[pick_base + 2 * block + 1]
        return partials_ref[first] + partials_ref[second]

    pl.semaphore_wait(barrier, pair_count - 1)

    def outgoing(peer):
        return pltpu.make_async_remote_copy(
            src_ref=send_ref.at[peer],
            dst_ref=recv_ref.at[me],
            send_sem=send_sems.at[peer],
            recv_sem=recv_sems.at[me],
            device_id=(row, peer),
            device_id_type=mesh_ids,
        )

    def send(step, carry):
        peer = lax.rem(me + step, pair_count)
        for part in range(owned):
            send_ref[peer, part] = block_sum(peer, part).astype(send_ref.dtype)
        outgoing(peer).start()
        return carry

    lax.fori_loop(1, pair_count, send, 0)

    def gather(step, total):
        peer = lax.rem(me + pair_count - step, pair_count)
        incoming = pltpu.make_async_remote_copy(
            src_ref=send_ref.at[peer],
            dst_ref=recv_ref.at[peer],
            send_sem=send_sems.at[peer],
            recv_sem=recv_sems.at[peer],
            device_id=(row, peer),
            device_id_type=mesh_ids,
        )
        incoming.wait_recv()
        return total + recv_ref[peer].astype(jnp.float32)

    own = jnp.stack([block_sum(me, part) for part in range(owned)])
    total = lax.fori_loop(1, pair_count, gather, own)

    def finish(step, carry):
        outgoing(lax.rem(me + step, pair_count)).wait_send()
        return carry

    lax.fori_loop(1, pair_count, finish, 0)
    out_ref[...] = total


def local(
    mode_fields, raman_taps, pair_blocks, light_blocks, target_blocks, raman_values, live_slots
):
    toeplitz = toeplitz_table(raman_taps)
    tap_count = toeplitz.shape[1]
    block_size = MB
    tm_count = lax.axis_size("tm")
    pair_count = lax.axis_size("pair")
    slot_count = pair_blocks.shape[1]
    entries = light_blocks.shape[2]
    mode_count = mode_fields.shape[1]
    length = mode_fields.shape[2]
    blocks = mode_count // block_size
    owned = blocks // pair_count
    rows = slot_count * entries
    halo = lax.ppermute(
        mode_fields[:, :, -tap_count:], "tm", [(k, k + 1) for k in range(tm_count - 1)]
    )
    halo = halo.reshape(2, blocks, block_size, tap_count)
    fields = mode_fields.reshape(2, blocks, block_size, length)
    square = block_size * block_size
    values = raman_values[0].reshape(slot_count, entries, square, square)
    row_index = jnp.arange(rows, dtype=jnp.int32)
    live_rows = row_index // entries < live_slots[0]
    feeds = (target_blocks.reshape(1, rows) == jnp.arange(blocks, dtype=jnp.int32)[:, None]) & live_rows[None]
    first = jnp.min(jnp.where(feeds, row_index[None], rows), axis=1)
    last = jnp.max(jnp.where(feeds, row_index[None], -1), axis=1)
    second = jnp.where(last > first, last, rows)
    ints = jnp.concatenate(
        [pair_blocks.reshape(-1), light_blocks.reshape(-1), jnp.stack([first, second], 1).reshape(-1)]
    )
    smem = pl.BlockSpec(memory_space=pltpu.SMEM)
    vmem = pl.BlockSpec(memory_space=pltpu.VMEM)
    exchange_shape = (pair_count, owned, 2, block_size, length)
    shared = pl.pallas_call(
        functools.partial(fused_kernel, slot_count, entries),
        out_shape=jax.ShapeDtypeStruct((owned, 2, block_size, length), jnp.float32),
        in_specs=[smem, vmem, vmem, vmem, vmem],
        out_specs=vmem,
        scratch_shapes=[
            pltpu.VMEM((rows + 1, 2, block_size, length), jnp.float32),
            pltpu.VMEM(exchange_shape, jnp.bfloat16),
            pltpu.VMEM(exchange_shape, jnp.bfloat16),
            pltpu.SemaphoreType.DMA((pair_count,)),
            pltpu.SemaphoreType.DMA((pair_count,)),
        ],
        compiler_params=pltpu.CompilerParams(collective_id=0, has_side_effects=True),
    )(ints, halo, fields, toeplitz, values)
    result = jnp.transpose(shared, (1, 0, 2, 3)).reshape(2, owned * block_size, length)
    return result


def solution(mesh):
    return jax.shard_map(
        local,
        mesh=mesh,
        in_specs=(
            P(None, None, "tm"),
            P(),
            P("pair", None, None),
            P("pair", None, None),
            P("pair", None),
            P("pair", None, None, None),
            P("pair"),
        ),
        out_specs=P(None, "pair", "tm"),
        check_vma=False,
    )
```

```python
import functools

import jax
import jax.numpy as jnp
from jax import lax
from jax.sharding import PartitionSpec as P
from jax.experimental import pallas as pl
from jax.experimental.pallas import tpu as pltpu

MB = 8


def toeplitz_table(tap_values):
    tap_count = tap_values.shape[0]
    rows = 2 * tap_count
    period = rows + tap_count
    zeros = jnp.zeros((rows,), tap_values.dtype)
    base = jnp.concatenate([tap_values[tap_count - 1:], zeros, tap_values[: tap_count - 1]])
    tiled = jnp.tile(base, rows)[: rows * (period - 1)].reshape(rows, period - 1)
    return tiled[:, :tap_count]


def fused_kernel(
    slot_count, entries, halves,
    ints_ref, halo_ref, fields_ref, table_ref, values_ref, out_ref,
    partials_ref, send_ref, recv_ref, send_sems, recv_sems,
):
    block_size = fields_ref.shape[2]
    length = fields_ref.shape[3]
    span_length = length // halves
    tap_count = halo_ref.shape[3]
    width = span_length + tap_count
    square = block_size * block_size
    pair_count = send_ref.shape[1]
    owned = send_ref.shape[2]
    light_base = 2 * slot_count
    pick_base = light_base + entries * slot_count
    zero_row = slot_count * entries
    me = lax.axis_index("pair")
    row = lax.axis_index("tm")
    mesh_ids = pl.DeviceIdType.MESH
    barrier = pltpu.get_barrier_semaphore()

    def greet(step, carry):
        peer = lax.rem(me + step, pair_count)
        pl.semaphore_signal(barrier, inc=1, device_id=(row, peer), device_id_type=mesh_ids)
        return carry

    lax.fori_loop(1, pair_count, greet, 0)

    table = table_ref[...]

    def window(part, block, half):
        if half == 0:
            head = halo_ref[part, block]
        else:
            head = fields_ref[part, block, :, pl.ds(half * span_length - tap_count, tap_count)]
        tail = fields_ref[part, block, :, pl.ds(half * span_length, span_length)]
        return jnp.concatenate([head, tail], 1).astype(jnp.float32)

    def compute(half):
        partials_ref[half, zero_row] = jnp.zeros(partials_ref.shape[2:], partials_ref.dtype)

        def body(slot_index, carry):
            left = ints_ref[2 * slot_index]
            right = ints_ref[2 * slot_index + 1]
            left_real = window(0, left, half)[:, None]
            left_imag = window(1, left, half)[:, None]
            right_real = window(0, right, half)[None]
            right_imag = window(1, right, half)[None]
            real_part = (left_real * right_real + left_imag * right_imag).reshape(square, width)
            imag_part = (left_imag * right_real - left_real * right_imag).reshape(square, width)
            intensity = jnp.concatenate([real_part, imag_part], 0).astype(jnp.bfloat16)
            pieces = []
            for piece in range(span_length // tap_count):
                span = intensity[:, piece * tap_count:piece * tap_count + 2 * tap_count]
                pieces.append(jnp.dot(span, table, preferred_element_type=jnp.float32))
            response = jnp.concatenate(pieces, 1).astype(jnp.bfloat16)
            for entry_index in range(entries):
                matrix = values_ref[slot_index, entry_index]
                mixed_real = jnp.dot(matrix, response[:square], preferred_element_type=jnp.float32).reshape(
                    block_size, block_size, span_length
                )
                mixed_imag = jnp.dot(matrix, response[square:], preferred_element_type=jnp.float32).reshape(
                    block_size, block_size, span_length
                )
                light = ints_ref[light_base + entries * slot_index + entry_index]
                columns = pl.ds(half * span_length, span_length)
                light_real = fields_ref[0, light, :, columns].astype(jnp.float32)[None]
                light_imag = fields_ref[1, light, :, columns].astype(jnp.float32)[None]
                out_real = jnp.sum(light_real * mixed_real - light_imag * mixed_imag, axis=1)
                out_imag = jnp.sum(light_real * mixed_imag + light_imag * mixed_real, axis=1)
                partials_ref[half, entries * slot_index + entry_index, 0] = out_real
                partials_ref[half, entries * slot_index + entry_index, 1] = out_imag
            return carry

        lax.fori_loop(0, slot_count, body, 0)

    def block_sum(half, peer, part):
        block = peer * owned + part
        first = ints_ref[pick_base + 2 * block]
        second = ints_ref[pick_base + 2 * block + 1]
        return partials_ref[half, first] + partials_ref[half, second]

    def copy_of(half, peer, source):
        return pltpu.make_async_remote_copy(
            src_ref=send_ref.at[half, peer],
            dst_ref=recv_ref.at[half, source],
            send_sem=send_sems.at[half, peer],
            recv_sem=recv_sems.at[half, source],
            device_id=(row, peer),
            device_id_type=mesh_ids,
        )

    def send_half(half):
        def send(step, carry):
            peer = lax.rem(me + step, pair_count)
            for part in range(owned):
                send_ref[half, peer, part] = block_sum(half, peer, part).astype(send_ref.dtype)
            copy_of(half, peer, me).start()
            return carry

        lax.fori_loop(1, pair_count, send, 0)

    for half in range(halves):
        compute(half)
        if half == 0:
            pl.semaphore_wait(barrier, pair_count - 1)
        send_half(half)

    for half in range(halves):
        def gather(step, total):
            peer = lax.rem(me + pair_count - step, pair_count)
            copy_of(half, peer, peer).wait_recv()
            return total + recv_ref[half, peer].astype(jnp.float32)

        own = jnp.stack([block_sum(half, me, part) for part in range(owned)])
        total = lax.fori_loop(1, pair_count, gather, own)
        out_ref[:, :, :, pl.ds(half * span_length, span_length)] = total

    for half in range(halves):
        def finish(step, carry):
            copy_of(half, lax.rem(me + step, pair_count), me).wait_send()
            return carry

        lax.fori_loop(1, pair_count, finish, 0)


def local(
    mode_fields, raman_taps, pair_blocks, light_blocks, target_blocks, raman_values, live_slots
):
    toeplitz = toeplitz_table(raman_taps)
    tap_count = toeplitz.shape[1]
    block_size = MB
    tm_count = lax.axis_size("tm")
    pair_count = lax.axis_size("pair")
    slot_count = pair_blocks.shape[1]
    entries = light_blocks.shape[2]
    mode_count = mode_fields.shape[1]
    length = mode_fields.shape[2]
    blocks = mode_count // block_size
    owned = blocks // pair_count
    rows = slot_count * entries
    halo = lax.ppermute(
        mode_fields[:, :, -tap_count:], "tm", [(k, k + 1) for k in range(tm_count - 1)]
    )
    halo = halo.reshape(2, blocks, block_size, tap_count)
    fields = mode_fields.reshape(2, blocks, block_size, length)
    square = block_size * block_size
    values = raman_values[0].reshape(slot_count, entries, square, square)
    row_index = jnp.arange(rows, dtype=jnp.int32)
    live_rows = row_index // entries < live_slots[0]
    feeds = (target_blocks.reshape(1, rows) == jnp.arange(blocks, dtype=jnp.int32)[:, None]) & live_rows[None]
    first = jnp.min(jnp.where(feeds, row_index[None], rows), axis=1)
    last = jnp.max(jnp.where(feeds, row_index[None], -1), axis=1)
    second = jnp.where(last > first, last, rows)
    ints = jnp.concatenate(
        [pair_blocks.reshape(-1), light_blocks.reshape(-1), jnp.stack([first, second], 1).reshape(-1)]
    )
    smem = pl.BlockSpec(memory_space=pltpu.SMEM)
    vmem = pl.BlockSpec(memory_space=pltpu.VMEM)
    halves = 2
    span_length = length // halves
    exchange_shape = (halves, pair_count, owned, 2, block_size, span_length)
    shared = pl.pallas_call(
        functools.partial(fused_kernel, slot_count, entries, halves),
        out_shape=jax.ShapeDtypeStruct((owned, 2, block_size, length), jnp.float32),
        in_specs=[smem, vmem, vmem, vmem, vmem],
        out_specs=vmem,
        scratch_shapes=[
            pltpu.VMEM((halves, rows + 1, 2, block_size, span_length), jnp.float32),
            pltpu.VMEM(exchange_shape, jnp.bfloat16),
            pltpu.VMEM(exchange_shape, jnp.bfloat16),
            pltpu.SemaphoreType.DMA((halves, pair_count)),
            pltpu.SemaphoreType.DMA((halves, pair_count)),
        ],
        compiler_params=pltpu.CompilerParams(collective_id=0, has_side_effects=True),
    )(ints, halo, fields, toeplitz, values)
    result = jnp.transpose(shared, (1, 0, 2, 3)).reshape(2, owned * block_size, length)
    return result


def solution(mesh):
    return jax.shard_map(
        local,
        mesh=mesh,
        in_specs=(
            P(None, None, "tm"),
            P(),
            P("pair", None, None),
            P("pair", None, None),
            P("pair", None),
            P("pair", None, None, None),
            P("pair"),
        ),
        out_specs=P(None, "pair", "tm"),
        check_vma=False,
    )
```

```python
import functools

import jax
import jax.numpy as jnp
from jax import lax
from jax.sharding import PartitionSpec as P
from jax.experimental import pallas as pl
from jax.experimental.pallas import tpu as pltpu

MB = 8


def fused_kernel(
    slot_count, entries,
    ints_ref, halo_ref, fields_ref, table_ref, values_ref, out_ref,
    partials_ref, send_ref, recv_ref, send_sems, recv_sems,
):
    block_size = fields_ref.shape[2]
    length = fields_ref.shape[3]
    tap_count = halo_ref.shape[3]
    width = length + tap_count
    square = block_size * block_size
    pair_count = send_ref.shape[0]
    owned = send_ref.shape[1]
    light_base = 2 * slot_count
    pick_base = light_base + entries * slot_count
    zero_row = slot_count * entries
    me = lax.axis_index("pair")
    row = lax.axis_index("tm")
    mesh_ids = pl.DeviceIdType.MESH
    barrier = pltpu.get_barrier_semaphore()

    def greet(step, carry):
        peer = lax.rem(me + step, pair_count)
        pl.semaphore_signal(barrier, inc=1, device_id=(row, peer), device_id_type=mesh_ids)
        return carry

    lax.fori_loop(1, pair_count, greet, 0)

    partials_ref[zero_row] = jnp.zeros(partials_ref.shape[1:], partials_ref.dtype)
    tap_count = halo_ref.shape[3]
    taps = table_ref[...].astype(jnp.float32)
    padded = jnp.concatenate([taps, jnp.zeros((1, 2 * tap_count), jnp.float32)], 1)
    spread = jnp.broadcast_to(padded, (2 * tap_count, 3 * tap_count))
    rolled = pltpu.roll(spread, 2 * tap_count + 1, 1, stride=1, stride_axis=0)
    table = rolled[:, :tap_count].astype(jnp.bfloat16)

    def window(part, block):
        return jnp.concatenate([halo_ref[part, block], fields_ref[part, block]], 1).astype(jnp.float32)

    def body(slot_index, carry):
        left = ints_ref[2 * slot_index]
        right = ints_ref[2 * slot_index + 1]
        left_real = window(0, left)[:, None]
        left_imag = window(1, left)[:, None]
        right_real = window(0, right)[None]
        right_imag = window(1, right)[None]
        real_part = (left_real * right_real + left_imag * right_imag).reshape(square, width)
        imag_part = (left_imag * right_real - left_real * right_imag).reshape(square, width)
        intensity = jnp.concatenate([real_part, imag_part], 0).astype(jnp.bfloat16)
        pieces = []
        for piece in range(length // tap_count):
            span = intensity[:, piece * tap_count:piece * tap_count + 2 * tap_count]
            pieces.append(jnp.dot(span, table, preferred_element_type=jnp.float32))
        response = jnp.concatenate(pieces, 1).astype(jnp.bfloat16)
        for entry_index in range(entries):
            matrix = values_ref[slot_index, entry_index]
            mixed_real = jnp.dot(matrix, response[:square], preferred_element_type=jnp.float32).reshape(
                block_size, block_size, length
            )
            mixed_imag = jnp.dot(matrix, response[square:], preferred_element_type=jnp.float32).reshape(
                block_size, block_size, length
            )
            light = ints_ref[light_base + entries * slot_index + entry_index]
            light_real = fields_ref[0, light].astype(jnp.float32)[None]
            light_imag = fields_ref[1, light].astype(jnp.float32)[None]
            out_real = jnp.sum(light_real * mixed_real - light_imag * mixed_imag, axis=1)
            out_imag = jnp.sum(light_real * mixed_imag + light_imag * mixed_real, axis=1)
            partials_ref[entries * slot_index + entry_index, 0] = out_real
            partials_ref[entries * slot_index + entry_index, 1] = out_imag
        return carry

    lax.fori_loop(0, slot_count, body, 0)

    def block_sum(peer, part):
        block = peer * owned + part
        first = ints_ref[pick_base + 2 * block]
        second = ints_ref[pick_base + 2 * block + 1]
        return partials_ref[first] + partials_ref[second]

    pl.semaphore_wait(barrier, pair_count - 1)

    def outgoing(peer):
        return pltpu.make_async_remote_copy(
            src_ref=send_ref.at[peer],
            dst_ref=recv_ref.at[me],
            send_sem=send_sems.at[peer],
            recv_sem=recv_sems.at[me],
            device_id=(row, peer),
            device_id_type=mesh_ids,
        )

    def send(step, carry):
        peer = lax.rem(me + step, pair_count)
        for part in range(owned):
            send_ref[peer, part] = block_sum(peer, part).astype(send_ref.dtype)
        outgoing(peer).start()
        return carry

    lax.fori_loop(1, pair_count, send, 0)

    def gather(step, total):
        peer = lax.rem(me + pair_count - step, pair_count)
        incoming = pltpu.make_async_remote_copy(
            src_ref=send_ref.at[peer],
            dst_ref=recv_ref.at[peer],
            send_sem=send_sems.at[peer],
            recv_sem=recv_sems.at[peer],
            device_id=(row, peer),
            device_id_type=mesh_ids,
        )
        incoming.wait_recv()
        return total + recv_ref[peer].astype(jnp.float32)

    own = jnp.stack([block_sum(me, part) for part in range(owned)])
    total = lax.fori_loop(1, pair_count, gather, own)

    def finish(step, carry):
        outgoing(lax.rem(me + step, pair_count)).wait_send()
        return carry

    lax.fori_loop(1, pair_count, finish, 0)
    out_ref[...] = total


def local(
    mode_fields, raman_taps, pair_blocks, light_blocks, target_blocks, raman_values, live_slots
):
    tap_count = raman_taps.shape[0]
    block_size = MB
    tm_count = lax.axis_size("tm")
    pair_count = lax.axis_size("pair")
    slot_count = pair_blocks.shape[1]
    entries = light_blocks.shape[2]
    mode_count = mode_fields.shape[1]
    length = mode_fields.shape[2]
    blocks = mode_count // block_size
    owned = blocks // pair_count
    rows = slot_count * entries
    halo = lax.ppermute(
        mode_fields[:, :, -tap_count:], "tm", [(k, k + 1) for k in range(tm_count - 1)]
    )
    halo = halo.reshape(2, blocks, block_size, tap_count)
    fields = mode_fields.reshape(2, blocks, block_size, length)
    square = block_size * block_size
    values = raman_values[0].reshape(slot_count, entries, square, square)
    row_index = jnp.arange(rows, dtype=jnp.int32)
    live_rows = row_index // entries < live_slots[0]
    feeds = (target_blocks.reshape(1, rows) == jnp.arange(blocks, dtype=jnp.int32)[:, None]) & live_rows[None]
    first = jnp.min(jnp.where(feeds, row_index[None], rows), axis=1)
    last = jnp.max(jnp.where(feeds, row_index[None], -1), axis=1)
    second = jnp.where(last > first, last, rows)
    ints = jnp.concatenate(
        [pair_blocks.reshape(-1), light_blocks.reshape(-1), jnp.stack([first, second], 1).reshape(-1)]
    )
    smem = pl.BlockSpec(memory_space=pltpu.SMEM)
    vmem = pl.BlockSpec(memory_space=pltpu.VMEM)
    exchange_shape = (pair_count, owned, 2, block_size, length)
    shared = pl.pallas_call(
        functools.partial(fused_kernel, slot_count, entries),
        out_shape=jax.ShapeDtypeStruct((owned, 2, block_size, length), jnp.float32),
        in_specs=[smem, vmem, vmem, vmem, vmem],
        out_specs=vmem,
        scratch_shapes=[
            pltpu.VMEM((rows + 1, 2, block_size, length), jnp.float32),
            pltpu.VMEM(exchange_shape, jnp.bfloat16),
            pltpu.VMEM(exchange_shape, jnp.bfloat16),
            pltpu.SemaphoreType.DMA((pair_count,)),
            pltpu.SemaphoreType.DMA((pair_count,)),
        ],
        compiler_params=pltpu.CompilerParams(collective_id=0, has_side_effects=True),
    )(ints, halo, fields, raman_taps.reshape(1, tap_count), values)
    result = jnp.transpose(shared, (1, 0, 2, 3)).reshape(2, owned * block_size, length)
    return result


def solution(mesh):
    return jax.shard_map(
        local,
        mesh=mesh,
        in_specs=(
            P(None, None, "tm"),
            P(),
            P("pair", None, None),
            P("pair", None, None),
            P("pair", None),
            P("pair", None, None, None),
            P("pair"),
        ),
        out_specs=P(None, "pair", "tm"),
        check_vma=False,
    )
```

```python
import functools

import jax
import jax.numpy as jnp
from jax import lax
from jax.sharding import PartitionSpec as P
from jax.experimental import pallas as pl
from jax.experimental.pallas import tpu as pltpu

MB = 8


def fused_kernel(
    slot_count, entries,
    pairs_ref, lights_ref, picks_ref, halo_ref, fields_ref, table_ref, values_ref, out_ref,
    partials_ref, send_ref, recv_ref, send_sems, recv_sems,
):
    block_size = fields_ref.shape[2]
    length = fields_ref.shape[3]
    tap_count = halo_ref.shape[3]
    width = length + tap_count
    square = block_size * block_size
    pair_count = send_ref.shape[0]
    owned = send_ref.shape[1]
    zero_row = slot_count * entries
    me = lax.axis_index("pair")
    row = lax.axis_index("tm")
    mesh_ids = pl.DeviceIdType.MESH
    barrier = pltpu.get_barrier_semaphore()

    def greet(step, carry):
        peer = lax.rem(me + step, pair_count)
        pl.semaphore_signal(barrier, inc=1, device_id=(row, peer), device_id_type=mesh_ids)
        return carry

    lax.fori_loop(1, pair_count, greet, 0)

    partials_ref[zero_row] = jnp.zeros(partials_ref.shape[1:], partials_ref.dtype)
    tap_count = halo_ref.shape[3]
    taps = table_ref[...].astype(jnp.float32)
    padded = jnp.concatenate([taps, jnp.zeros((1, 2 * tap_count), jnp.float32)], 1)
    spread = jnp.broadcast_to(padded, (2 * tap_count, 3 * tap_count))
    rolled = pltpu.roll(spread, 2 * tap_count + 1, 1, stride=1, stride_axis=0)
    table = rolled[:, :tap_count].astype(jnp.bfloat16)

    def window(part, block):
        return jnp.concatenate([halo_ref[part, block], fields_ref[part, block]], 1).astype(jnp.float32)

    def body(slot_index, carry):
        left = pairs_ref[0, slot_index, 0]
        right = pairs_ref[0, slot_index, 1]
        left_real = window(0, left)[:, None]
        left_imag = window(1, left)[:, None]
        right_real = window(0, right)[None]
        right_imag = window(1, right)[None]
        real_part = (left_real * right_real + left_imag * right_imag).reshape(square, width)
        imag_part = (left_imag * right_real - left_real * right_imag).reshape(square, width)
        intensity = jnp.concatenate([real_part, imag_part], 0).astype(jnp.bfloat16)
        pieces = []
        for piece in range(length // tap_count):
            span = intensity[:, piece * tap_count:piece * tap_count + 2 * tap_count]
            pieces.append(jnp.dot(span, table, preferred_element_type=jnp.float32))
        response = jnp.concatenate(pieces, 1).astype(jnp.bfloat16)
        for entry_index in range(entries):
            matrix = values_ref[slot_index, entry_index]
            mixed_real = jnp.dot(matrix, response[:square], preferred_element_type=jnp.float32).reshape(
                block_size, block_size, length
            )
            mixed_imag = jnp.dot(matrix, response[square:], preferred_element_type=jnp.float32).reshape(
                block_size, block_size, length
            )
            light = lights_ref[0, slot_index, entry_index]
            light_real = fields_ref[0, light].astype(jnp.float32)[None]
            light_imag = fields_ref[1, light].astype(jnp.float32)[None]
            out_real = jnp.sum(light_real * mixed_real - light_imag * mixed_imag, axis=1)
            out_imag = jnp.sum(light_real * mixed_imag + light_imag * mixed_real, axis=1)
            partials_ref[entries * slot_index + entry_index, 0] = out_real
            partials_ref[entries * slot_index + entry_index, 1] = out_imag
        return carry

    lax.fori_loop(0, slot_count, body, 0)

    def block_sum(peer, part):
        block = peer * owned + part
        first = picks_ref[block, 0]
        second = picks_ref[block, 1]
        return partials_ref[first] + partials_ref[second]

    pl.semaphore_wait(barrier, pair_count - 1)

    def outgoing(peer):
        return pltpu.make_async_remote_copy(
            src_ref=send_ref.at[peer],
            dst_ref=recv_ref.at[me],
            send_sem=send_sems.at[peer],
            recv_sem=recv_sems.at[me],
            device_id=(row, peer),
            device_id_type=mesh_ids,
        )

    def send(step, carry):
        peer = lax.rem(me + step, pair_count)
        for part in range(owned):
            send_ref[peer, part] = block_sum(peer, part).astype(send_ref.dtype)
        outgoing(peer).start()
        return carry

    lax.fori_loop(1, pair_count, send, 0)

    def gather(step, total):
        peer = lax.rem(me + pair_count - step, pair_count)
        incoming = pltpu.make_async_remote_copy(
            src_ref=send_ref.at[peer],
            dst_ref=recv_ref.at[peer],
            send_sem=send_sems.at[peer],
            recv_sem=recv_sems.at[peer],
            device_id=(row, peer),
            device_id_type=mesh_ids,
        )
        incoming.wait_recv()
        return total + recv_ref[peer].astype(jnp.float32)

    own = jnp.stack([block_sum(me, part) for part in range(owned)])
    total = lax.fori_loop(1, pair_count, gather, own)

    def finish(step, carry):
        outgoing(lax.rem(me + step, pair_count)).wait_send()
        return carry

    lax.fori_loop(1, pair_count, finish, 0)
    out_ref[...] = total


def local(
    mode_fields, raman_taps, pair_blocks, light_blocks, target_blocks, raman_values, live_slots
):
    tap_count = raman_taps.shape[0]
    block_size = MB
    tm_count = lax.axis_size("tm")
    pair_count = lax.axis_size("pair")
    slot_count = pair_blocks.shape[1]
    entries = light_blocks.shape[2]
    mode_count = mode_fields.shape[1]
    length = mode_fields.shape[2]
    blocks = mode_count // block_size
    owned = blocks // pair_count
    rows = slot_count * entries
    halo = lax.ppermute(
        mode_fields[:, :, -tap_count:], "tm", [(k, k + 1) for k in range(tm_count - 1)]
    )
    halo = halo.reshape(2, blocks, block_size, tap_count)
    fields = mode_fields.reshape(2, blocks, block_size, length)
    square = block_size * block_size
    values = raman_values[0].reshape(slot_count, entries, square, square)
    row_index = jnp.arange(rows, dtype=jnp.int32)
    live_rows = row_index // entries < live_slots[0]
    feeds = (target_blocks.reshape(1, rows) == jnp.arange(blocks, dtype=jnp.int32)[:, None]) & live_rows[None]
    first = jnp.min(jnp.where(feeds, row_index[None], rows), axis=1)
    last = jnp.max(jnp.where(feeds, row_index[None], -1), axis=1)
    second = jnp.where(last > first, last, rows)
    picks = jnp.stack([first, second], 1)
    smem = pl.BlockSpec(memory_space=pltpu.SMEM)
    vmem = pl.BlockSpec(memory_space=pltpu.VMEM)
    exchange_shape = (pair_count, owned, 2, block_size, length)
    shared = pl.pallas_call(
        functools.partial(fused_kernel, slot_count, entries),
        out_shape=jax.ShapeDtypeStruct((owned, 2, block_size, length), jnp.float32),
        in_specs=[smem, smem, smem, vmem, vmem, vmem, vmem],
        out_specs=vmem,
        scratch_shapes=[
            pltpu.VMEM((rows + 1, 2, block_size, length), jnp.float32),
            pltpu.VMEM(exchange_shape, jnp.bfloat16),
            pltpu.VMEM(exchange_shape, jnp.bfloat16),
            pltpu.SemaphoreType.DMA((pair_count,)),
            pltpu.SemaphoreType.DMA((pair_count,)),
        ],
        compiler_params=pltpu.CompilerParams(collective_id=0, has_side_effects=True),
    )(pair_blocks, light_blocks, picks, halo, fields, raman_taps.reshape(1, tap_count), values)
    result = jnp.transpose(shared, (1, 0, 2, 3)).reshape(2, owned * block_size, length)
    return result


def solution(mesh):
    return jax.shard_map(
        local,
        mesh=mesh,
        in_specs=(
            P(None, None, "tm"),
            P(),
            P("pair", None, None),
            P("pair", None, None),
            P("pair", None),
            P("pair", None, None, None),
            P("pair"),
        ),
        out_specs=P(None, "pair", "tm"),
        check_vma=False,
    )
```

```python
import functools

import jax
import jax.numpy as jnp
from jax import lax
from jax.sharding import PartitionSpec as P
from jax.experimental import pallas as pl
from jax.experimental.pallas import tpu as pltpu

MB = 8


def fused_kernel(
    slot_count, entries,
    ints_ref, halo_ref, fields_ref, table_ref, values_ref, out_ref,
    partials_ref, send_ref, recv_ref, send_sems, recv_sems,
):
    block_size = fields_ref.shape[2]
    length = fields_ref.shape[3]
    tap_count = halo_ref.shape[3]
    width = length + tap_count
    square = block_size * block_size
    pair_count = send_ref.shape[0]
    owned = send_ref.shape[1]
    light_base = 2 * slot_count
    pick_base = light_base + entries * slot_count
    zero_row = slot_count * entries
    me = lax.axis_index("pair")
    row = lax.axis_index("tm")
    mesh_ids = pl.DeviceIdType.MESH
    barrier = pltpu.get_barrier_semaphore()

    def greet(step, carry):
        peer = lax.rem(me + step, pair_count)
        pl.semaphore_signal(barrier, inc=1, device_id=(row, peer), device_id_type=mesh_ids)
        return carry

    lax.fori_loop(1, pair_count, greet, 0)

    partials_ref[zero_row] = jnp.zeros(partials_ref.shape[1:], partials_ref.dtype)
    tap_count = halo_ref.shape[3]
    taps = table_ref[...].astype(jnp.float32)
    padded = jnp.concatenate([taps, jnp.zeros((1, 2 * tap_count), jnp.float32)], 1)
    spread = jnp.broadcast_to(padded, (2 * tap_count, 3 * tap_count))
    rolled = pltpu.roll(spread, 2 * tap_count + 1, 1, stride=1, stride_axis=0)
    table = rolled[:, :tap_count].astype(jnp.bfloat16)

    def window(part, block):
        return jnp.concatenate([halo_ref[part, block], fields_ref[part, block]], 1).astype(jnp.float32)

    def body(slot_index, carry):
        left = ints_ref[2 * slot_index]
        right = ints_ref[2 * slot_index + 1]
        left_real = window(0, left)[:, None]
        left_imag = window(1, left)[:, None]
        right_real = window(0, right)[None]
        right_imag = window(1, right)[None]
        real_part = (left_real * right_real + left_imag * right_imag).reshape(square, width)
        imag_part = (left_imag * right_real - left_real * right_imag).reshape(square, width)
        intensity = jnp.concatenate([real_part, imag_part], 0).astype(jnp.bfloat16)
        pieces = []
        for piece in range(length // tap_count):
            span = intensity[:, piece * tap_count:piece * tap_count + 2 * tap_count]
            pieces.append(jnp.dot(span, table, preferred_element_type=jnp.float32))
        response = jnp.concatenate(pieces, 1).astype(jnp.bfloat16)
        for entry_index in range(entries):
            matrix = values_ref[slot_index, entry_index]
            mixed_real = jnp.dot(matrix, response[:square], preferred_element_type=jnp.float32).reshape(
                block_size, block_size, length
            )
            mixed_imag = jnp.dot(matrix, response[square:], preferred_element_type=jnp.float32).reshape(
                block_size, block_size, length
            )
            light = ints_ref[light_base + entries * slot_index + entry_index]
            light_real = fields_ref[0, light].astype(jnp.float32)[None]
            light_imag = fields_ref[1, light].astype(jnp.float32)[None]
            out_real = jnp.sum(light_real * mixed_real - light_imag * mixed_imag, axis=1)
            out_imag = jnp.sum(light_real * mixed_imag + light_imag * mixed_real, axis=1)
            partials_ref[entries * slot_index + entry_index, 0] = out_real
            partials_ref[entries * slot_index + entry_index, 1] = out_imag
        return carry

    lax.fori_loop(0, slot_count, body, 0, unroll=2)

    def block_sum(peer, part):
        block = peer * owned + part
        first = ints_ref[pick_base + 2 * block]
        second = ints_ref[pick_base + 2 * block + 1]
        return partials_ref[first] + partials_ref[second]

    pl.semaphore_wait(barrier, pair_count - 1)

    def outgoing(peer):
        return pltpu.make_async_remote_copy(
            src_ref=send_ref.at[peer],
            dst_ref=recv_ref.at[me],
            send_sem=send_sems.at[peer],
            recv_sem=recv_sems.at[me],
            device_id=(row, peer),
            device_id_type=mesh_ids,
        )

    def send(step, carry):
        peer = lax.rem(me + step, pair_count)
        for part in range(owned):
            send_ref[peer, part] = block_sum(peer, part).astype(send_ref.dtype)
        outgoing(peer).start()
        return carry

    lax.fori_loop(1, pair_count, send, 0)

    def gather(step, total):
        peer = lax.rem(me + pair_count - step, pair_count)
        incoming = pltpu.make_async_remote_copy(
            src_ref=send_ref.at[peer],
            dst_ref=recv_ref.at[peer],
            send_sem=send_sems.at[peer],
            recv_sem=recv_sems.at[peer],
            device_id=(row, peer),
            device_id_type=mesh_ids,
        )
        incoming.wait_recv()
        return total + recv_ref[peer].astype(jnp.float32)

    own = jnp.stack([block_sum(me, part) for part in range(owned)])
    total = lax.fori_loop(1, pair_count, gather, own)

    def finish(step, carry):
        outgoing(lax.rem(me + step, pair_count)).wait_send()
        return carry

    lax.fori_loop(1, pair_count, finish, 0)
    out_ref[...] = total


def local(
    mode_fields, raman_taps, pair_blocks, light_blocks, target_blocks, raman_values, live_slots
):
    tap_count = raman_taps.shape[0]
    block_size = MB
    tm_count = lax.axis_size("tm")
    pair_count = lax.axis_size("pair")
    slot_count = pair_blocks.shape[1]
    entries = light_blocks.shape[2]
    mode_count = mode_fields.shape[1]
    length = mode_fields.shape[2]
    blocks = mode_count // block_size
    owned = blocks // pair_count
    rows = slot_count * entries
    halo = lax.ppermute(
        mode_fields[:, :, -tap_count:], "tm", [(k, k + 1) for k in range(tm_count - 1)]
    )
    halo = halo.reshape(2, blocks, block_size, tap_count)
    fields = mode_fields.reshape(2, blocks, block_size, length)
    square = block_size * block_size
    values = raman_values[0].reshape(slot_count, entries, square, square)
    row_index = jnp.arange(rows, dtype=jnp.int32)
    live_rows = row_index // entries < live_slots[0]
    feeds = (target_blocks.reshape(1, rows) == jnp.arange(blocks, dtype=jnp.int32)[:, None]) & live_rows[None]
    first = jnp.min(jnp.where(feeds, row_index[None], rows), axis=1)
    last = jnp.max(jnp.where(feeds, row_index[None], -1), axis=1)
    second = jnp.where(last > first, last, rows)
    ints = jnp.concatenate(
        [pair_blocks.reshape(-1), light_blocks.reshape(-1), jnp.stack([first, second], 1).reshape(-1)]
    )
    smem = pl.BlockSpec(memory_space=pltpu.SMEM)
    vmem = pl.BlockSpec(memory_space=pltpu.VMEM)
    exchange_shape = (pair_count, owned, 2, block_size, length)
    shared = pl.pallas_call(
        functools.partial(fused_kernel, slot_count, entries),
        out_shape=jax.ShapeDtypeStruct((owned, 2, block_size, length), jnp.float32),
        in_specs=[smem, vmem, vmem, vmem, vmem],
        out_specs=vmem,
        scratch_shapes=[
            pltpu.VMEM((rows + 1, 2, block_size, length), jnp.float32),
            pltpu.VMEM(exchange_shape, jnp.bfloat16),
            pltpu.VMEM(exchange_shape, jnp.bfloat16),
            pltpu.SemaphoreType.DMA((pair_count,)),
            pltpu.SemaphoreType.DMA((pair_count,)),
        ],
        compiler_params=pltpu.CompilerParams(collective_id=0, has_side_effects=True),
    )(ints, halo, fields, raman_taps.reshape(1, tap_count), values)
    result = jnp.transpose(shared, (1, 0, 2, 3)).reshape(2, owned * block_size, length)
    return result


def solution(mesh):
    return jax.shard_map(
        local,
        mesh=mesh,
        in_specs=(
            P(None, None, "tm"),
            P(),
            P("pair", None, None),
            P("pair", None, None),
            P("pair", None),
            P("pair", None, None, None),
            P("pair"),
        ),
        out_specs=P(None, "pair", "tm"),
        check_vma=False,
    )
```

```python
import functools

import jax
import jax.numpy as jnp
from jax import lax
from jax.sharding import PartitionSpec as P
from jax.experimental import pallas as pl
from jax.experimental.pallas import tpu as pltpu

MB = 8


def fused_kernel(
    slot_count, entries,
    ints_ref, halo_ref, fields_ref, table_ref, values_ref, out_ref,
    partials_ref, send_ref, recv_ref, send_sems, recv_sems,
):
    block_size = fields_ref.shape[2]
    length = fields_ref.shape[3]
    tap_count = halo_ref.shape[3]
    width = length + tap_count
    square = block_size * block_size
    pair_count = send_ref.shape[0]
    owned = send_ref.shape[1]
    light_base = 2 * slot_count
    pick_base = light_base + entries * slot_count
    zero_row = slot_count * entries
    me = lax.axis_index("pair")
    row = lax.axis_index("tm")
    mesh_ids = pl.DeviceIdType.MESH
    barrier = pltpu.get_barrier_semaphore()

    def greet(step, carry):
        peer = lax.rem(me + step, pair_count)
        pl.semaphore_signal(barrier, inc=1, device_id=(row, peer), device_id_type=mesh_ids)
        return carry

    lax.fori_loop(1, pair_count, greet, 0)

    partials_ref[zero_row] = jnp.zeros(partials_ref.shape[1:], partials_ref.dtype)
    tap_count = halo_ref.shape[3]
    taps = table_ref[...].astype(jnp.float32)
    padded = jnp.concatenate([taps, jnp.zeros((1, 2 * tap_count), jnp.float32)], 1)
    spread = jnp.broadcast_to(padded, (2 * tap_count, 3 * tap_count))
    rolled = pltpu.roll(spread, 2 * tap_count + 1, 1, stride=1, stride_axis=0)
    table = rolled[:, :tap_count].astype(jnp.bfloat16)

    def window(part, block):
        return jnp.concatenate([halo_ref[part, block], fields_ref[part, block]], 1).astype(jnp.float32)

    def body(slot_index, carry):
        left = ints_ref[2 * slot_index]
        right = ints_ref[2 * slot_index + 1]
        left_real = window(0, left)[:, None]
        left_imag = window(1, left)[:, None]
        right_real = window(0, right)[None]
        right_imag = window(1, right)[None]
        real_part = (left_real * right_real + left_imag * right_imag).reshape(square, width)
        imag_part = (left_imag * right_real - left_real * right_imag).reshape(square, width)
        intensity = jnp.concatenate([real_part, imag_part], 0).astype(jnp.bfloat16)
        pieces = []
        for piece in range(length // tap_count):
            span = intensity[:, piece * tap_count:piece * tap_count + 2 * tap_count]
            pieces.append(jnp.dot(span, table, preferred_element_type=jnp.float32))
        response = jnp.concatenate(pieces, 1).astype(jnp.bfloat16)
        for entry_index in range(entries):
            matrix = values_ref[slot_index, entry_index]
            mixed_real = jnp.dot(matrix, response[:square], preferred_element_type=jnp.float32).reshape(
                block_size, block_size, length
            )
            mixed_imag = jnp.dot(matrix, response[square:], preferred_element_type=jnp.float32).reshape(
                block_size, block_size, length
            )
            light = ints_ref[light_base + entries * slot_index + entry_index]
            light_real = fields_ref[0, light].astype(jnp.float32)[None]
            light_imag = fields_ref[1, light].astype(jnp.float32)[None]
            out_real = jnp.sum(light_real * mixed_real - light_imag * mixed_imag, axis=1)
            out_imag = jnp.sum(light_real * mixed_imag + light_imag * mixed_real, axis=1)
            partials_ref[entries * slot_index + entry_index, 0] = out_real
            partials_ref[entries * slot_index + entry_index, 1] = out_imag
        return carry

    lax.fori_loop(0, slot_count, body, 0, unroll=4)

    def block_sum(peer, part):
        block = peer * owned + part
        first = ints_ref[pick_base + 2 * block]
        second = ints_ref[pick_base + 2 * block + 1]
        return partials_ref[first] + partials_ref[second]

    pl.semaphore_wait(barrier, pair_count - 1)

    def outgoing(peer):
        return pltpu.make_async_remote_copy(
            src_ref=send_ref.at[peer],
            dst_ref=recv_ref.at[me],
            send_sem=send_sems.at[peer],
            recv_sem=recv_sems.at[me],
            device_id=(row, peer),
            device_id_type=mesh_ids,
        )

    def send(step, carry):
        peer = lax.rem(me + step, pair_count)
        for part in range(owned):
            send_ref[peer, part] = block_sum(peer, part).astype(send_ref.dtype)
        outgoing(peer).start()
        return carry

    lax.fori_loop(1, pair_count, send, 0)

    def gather(step, total):
        peer = lax.rem(me + pair_count - step, pair_count)
        incoming = pltpu.make_async_remote_copy(
            src_ref=send_ref.at[peer],
            dst_ref=recv_ref.at[peer],
            send_sem=send_sems.at[peer],
            recv_sem=recv_sems.at[peer],
            device_id=(row, peer),
            device_id_type=mesh_ids,
        )
        incoming.wait_recv()
        return total + recv_ref[peer].astype(jnp.float32)

    own = jnp.stack([block_sum(me, part) for part in range(owned)])
    total = lax.fori_loop(1, pair_count, gather, own)

    def finish(step, carry):
        outgoing(lax.rem(me + step, pair_count)).wait_send()
        return carry

    lax.fori_loop(1, pair_count, finish, 0)
    out_ref[...] = total


def local(
    mode_fields, raman_taps, pair_blocks, light_blocks, target_blocks, raman_values, live_slots
):
    tap_count = raman_taps.shape[0]
    block_size = MB
    tm_count = lax.axis_size("tm")
    pair_count = lax.axis_size("pair")
    slot_count = pair_blocks.shape[1]
    entries = light_blocks.shape[2]
    mode_count = mode_fields.shape[1]
    length = mode_fields.shape[2]
    blocks = mode_count // block_size
    owned = blocks // pair_count
    rows = slot_count * entries
    halo = lax.ppermute(
        mode_fields[:, :, -tap_count:], "tm", [(k, k + 1) for k in range(tm_count - 1)]
    )
    halo = halo.reshape(2, blocks, block_size, tap_count)
    fields = mode_fields.reshape(2, blocks, block_size, length)
    square = block_size * block_size
    values = raman_values[0].reshape(slot_count, entries, square, square)
    row_index = jnp.arange(rows, dtype=jnp.int32)
    live_rows = row_index // entries < live_slots[0]
    feeds = (target_blocks.reshape(1, rows) == jnp.arange(blocks, dtype=jnp.int32)[:, None]) & live_rows[None]
    first = jnp.min(jnp.where(feeds, row_index[None], rows), axis=1)
    last = jnp.max(jnp.where(feeds, row_index[None], -1), axis=1)
    second = jnp.where(last > first, last, rows)
    ints = jnp.concatenate(
        [pair_blocks.reshape(-1), light_blocks.reshape(-1), jnp.stack([first, second], 1).reshape(-1)]
    )
    smem = pl.BlockSpec(memory_space=pltpu.SMEM)
    vmem = pl.BlockSpec(memory_space=pltpu.VMEM)
    exchange_shape = (pair_count, owned, 2, block_size, length)
    shared = pl.pallas_call(
        functools.partial(fused_kernel, slot_count, entries),
        out_shape=jax.ShapeDtypeStruct((owned, 2, block_size, length), jnp.float32),
        in_specs=[smem, vmem, vmem, vmem, vmem],
        out_specs=vmem,
        scratch_shapes=[
            pltpu.VMEM((rows + 1, 2, block_size, length), jnp.float32),
            pltpu.VMEM(exchange_shape, jnp.bfloat16),
            pltpu.VMEM(exchange_shape, jnp.bfloat16),
            pltpu.SemaphoreType.DMA((pair_count,)),
            pltpu.SemaphoreType.DMA((pair_count,)),
        ],
        compiler_params=pltpu.CompilerParams(collective_id=0, has_side_effects=True),
    )(ints, halo, fields, raman_taps.reshape(1, tap_count), values)
    result = jnp.transpose(shared, (1, 0, 2, 3)).reshape(2, owned * block_size, length)
    return result


def solution(mesh):
    return jax.shard_map(
        local,
        mesh=mesh,
        in_specs=(
            P(None, None, "tm"),
            P(),
            P("pair", None, None),
            P("pair", None, None),
            P("pair", None),
            P("pair", None, None, None),
            P("pair"),
        ),
        out_specs=P(None, "pair", "tm"),
        check_vma=False,
    )
```

```python
import functools

import jax
import jax.numpy as jnp
from jax import lax
from jax.sharding import PartitionSpec as P
from jax.experimental import pallas as pl
from jax.experimental.pallas import tpu as pltpu

MB = 8


def fused_kernel(
    slot_count, entries,
    ints_ref, halo_ref, fields_ref, table_ref, values_ref, out_ref,
    partials_ref, send_ref, recv_ref, send_sems, recv_sems,
):
    block_size = fields_ref.shape[2]
    length = fields_ref.shape[3]
    tap_count = halo_ref.shape[3]
    width = length + tap_count
    square = block_size * block_size
    pair_count = send_ref.shape[0]
    owned = send_ref.shape[1]
    light_base = 2 * slot_count
    pick_base = light_base + entries * slot_count
    zero_row = slot_count * entries
    me = lax.axis_index("pair")
    row = lax.axis_index("tm")
    mesh_ids = pl.DeviceIdType.MESH
    barrier = pltpu.get_barrier_semaphore()

    def greet(step, carry):
        peer = lax.rem(me + step, pair_count)
        pl.semaphore_signal(barrier, inc=1, device_id=(row, peer), device_id_type=mesh_ids)
        return carry

    lax.fori_loop(1, pair_count, greet, 0)

    partials_ref[zero_row] = jnp.zeros(partials_ref.shape[1:], partials_ref.dtype)
    tap_count = halo_ref.shape[3]
    taps = table_ref[...].astype(jnp.float32)
    padded = jnp.concatenate([taps, jnp.zeros((1, 2 * tap_count), jnp.float32)], 1)
    spread = jnp.broadcast_to(padded, (2 * tap_count, 3 * tap_count))
    rolled = pltpu.roll(spread, 2 * tap_count + 1, 1, stride=1, stride_axis=0)
    table = rolled[:, :tap_count].astype(jnp.bfloat16)

    def window(part, block):
        return jnp.concatenate([halo_ref[part, block], fields_ref[part, block]], 1).astype(jnp.float32)

    def body(slot_index, carry):
        left = ints_ref[2 * slot_index]
        right = ints_ref[2 * slot_index + 1]
        left_real = window(0, left)[:, None]
        left_imag = window(1, left)[:, None]
        right_real = window(0, right)[None]
        right_imag = window(1, right)[None]
        real_part = (left_real * right_real + left_imag * right_imag).reshape(square, width)
        imag_part = (left_imag * right_real - left_real * right_imag).reshape(square, width)
        intensity = jnp.concatenate([real_part, imag_part], 0).astype(jnp.bfloat16)
        pieces = []
        for piece in range(length // tap_count):
            span = intensity[:, piece * tap_count:piece * tap_count + 2 * tap_count]
            pieces.append(jnp.dot(span, table, preferred_element_type=jnp.float32))
        response = jnp.concatenate(pieces, 1).astype(jnp.bfloat16)
        for entry_index in range(entries):
            matrix = values_ref[slot_index, entry_index]
            mixed_real = jnp.dot(matrix, response[:square], preferred_element_type=jnp.float32).reshape(
                block_size, block_size, length
            )
            mixed_imag = jnp.dot(matrix, response[square:], preferred_element_type=jnp.float32).reshape(
                block_size, block_size, length
            )
            light = ints_ref[light_base + entries * slot_index + entry_index]
            light_real = fields_ref[0, light].astype(jnp.float32)[None]
            light_imag = fields_ref[1, light].astype(jnp.float32)[None]
            out_real = jnp.sum(light_real * mixed_real - light_imag * mixed_imag, axis=1)
            out_imag = jnp.sum(light_real * mixed_imag + light_imag * mixed_real, axis=1)
            partials_ref[entries * slot_index + entry_index, 0] = out_real
            partials_ref[entries * slot_index + entry_index, 1] = out_imag
        return carry

    lax.fori_loop(0, slot_count, body, 0, unroll=4)

    def block_sum(peer, part):
        block = peer * owned + part
        first = ints_ref[pick_base + 2 * block]
        second = ints_ref[pick_base + 2 * block + 1]
        return partials_ref[first] + partials_ref[second]

    pl.semaphore_wait(barrier, pair_count - 1)

    def outgoing(peer):
        return pltpu.make_async_remote_copy(
            src_ref=send_ref.at[peer],
            dst_ref=recv_ref.at[me],
            send_sem=send_sems.at[peer],
            recv_sem=recv_sems.at[me],
            device_id=(row, peer),
            device_id_type=mesh_ids,
        )

    def send(step, carry):
        peer = lax.rem(me + step, pair_count)
        for part in range(owned):
            send_ref[peer, part] = block_sum(peer, part).astype(send_ref.dtype)
        outgoing(peer).start()
        return carry

    lax.fori_loop(1, pair_count, send, 0, unroll=4)

    def gather(step, total):
        peer = lax.rem(me + pair_count - step, pair_count)
        incoming = pltpu.make_async_remote_copy(
            src_ref=send_ref.at[peer],
            dst_ref=recv_ref.at[peer],
            send_sem=send_sems.at[peer],
            recv_sem=recv_sems.at[peer],
            device_id=(row, peer),
            device_id_type=mesh_ids,
        )
        incoming.wait_recv()
        return total + recv_ref[peer].astype(jnp.float32)

    own = jnp.stack([block_sum(me, part) for part in range(owned)])
    total = lax.fori_loop(1, pair_count, gather, own, unroll=4)

    def finish(step, carry):
        outgoing(lax.rem(me + step, pair_count)).wait_send()
        return carry

    lax.fori_loop(1, pair_count, finish, 0)
    out_ref[...] = total


def local(
    mode_fields, raman_taps, pair_blocks, light_blocks, target_blocks, raman_values, live_slots
):
    tap_count = raman_taps.shape[0]
    block_size = MB
    tm_count = lax.axis_size("tm")
    pair_count = lax.axis_size("pair")
    slot_count = pair_blocks.shape[1]
    entries = light_blocks.shape[2]
    mode_count = mode_fields.shape[1]
    length = mode_fields.shape[2]
    blocks = mode_count // block_size
    owned = blocks // pair_count
    rows = slot_count * entries
    halo = lax.ppermute(
        mode_fields[:, :, -tap_count:], "tm", [(k, k + 1) for k in range(tm_count - 1)]
    )
    halo = halo.reshape(2, blocks, block_size, tap_count)
    fields = mode_fields.reshape(2, blocks, block_size, length)
    square = block_size * block_size
    values = raman_values[0].reshape(slot_count, entries, square, square)
    row_index = jnp.arange(rows, dtype=jnp.int32)
    live_rows = row_index // entries < live_slots[0]
    feeds = (target_blocks.reshape(1, rows) == jnp.arange(blocks, dtype=jnp.int32)[:, None]) & live_rows[None]
    first = jnp.min(jnp.where(feeds, row_index[None], rows), axis=1)
    last = jnp.max(jnp.where(feeds, row_index[None], -1), axis=1)
    second = jnp.where(last > first, last, rows)
    ints = jnp.concatenate(
        [pair_blocks.reshape(-1), light_blocks.reshape(-1), jnp.stack([first, second], 1).reshape(-1)]
    )
    smem = pl.BlockSpec(memory_space=pltpu.SMEM)
    vmem = pl.BlockSpec(memory_space=pltpu.VMEM)
    exchange_shape = (pair_count, owned, 2, block_size, length)
    shared = pl.pallas_call(
        functools.partial(fused_kernel, slot_count, entries),
        out_shape=jax.ShapeDtypeStruct((owned, 2, block_size, length), jnp.float32),
        in_specs=[smem, vmem, vmem, vmem, vmem],
        out_specs=vmem,
        scratch_shapes=[
            pltpu.VMEM((rows + 1, 2, block_size, length), jnp.float32),
            pltpu.VMEM(exchange_shape, jnp.bfloat16),
            pltpu.VMEM(exchange_shape, jnp.bfloat16),
            pltpu.SemaphoreType.DMA((pair_count,)),
            pltpu.SemaphoreType.DMA((pair_count,)),
        ],
        compiler_params=pltpu.CompilerParams(collective_id=0, has_side_effects=True),
    )(ints, halo, fields, raman_taps.reshape(1, tap_count), values)
    result = jnp.transpose(shared, (1, 0, 2, 3)).reshape(2, owned * block_size, length)
    return result


def solution(mesh):
    return jax.shard_map(
        local,
        mesh=mesh,
        in_specs=(
            P(None, None, "tm"),
            P(),
            P("pair", None, None),
            P("pair", None, None),
            P("pair", None),
            P("pair", None, None, None),
            P("pair"),
        ),
        out_specs=P(None, "pair", "tm"),
        check_vma=False,
    )
```

```python
import functools

import jax
import jax.numpy as jnp
from jax import lax
from jax.sharding import PartitionSpec as P
from jax.experimental import pallas as pl
from jax.experimental.pallas import tpu as pltpu

MB = 8


def fused_kernel(
    slot_count, entries,
    ints_ref, halo_ref, fields_ref, table_ref, values_ref, out_ref,
    partials_ref, send_ref, recv_ref, send_sems, recv_sems,
):
    block_size = fields_ref.shape[2]
    length = fields_ref.shape[3]
    tap_count = halo_ref.shape[3]
    width = length + tap_count
    square = block_size * block_size
    pair_count = send_ref.shape[0]
    owned = send_ref.shape[1]
    light_base = 2 * slot_count
    pick_base = light_base + entries * slot_count
    zero_row = slot_count * entries
    me = lax.axis_index("pair")
    row = lax.axis_index("tm")
    mesh_ids = pl.DeviceIdType.MESH
    barrier = pltpu.get_barrier_semaphore()

    def greet(step, carry):
        peer = lax.rem(me + step, pair_count)
        pl.semaphore_signal(barrier, inc=1, device_id=(row, peer), device_id_type=mesh_ids)
        return carry

    lax.fori_loop(1, pair_count, greet, 0)

    partials_ref[zero_row] = jnp.zeros(partials_ref.shape[1:], partials_ref.dtype)
    tap_count = halo_ref.shape[3]
    taps = table_ref[...].astype(jnp.float32)
    padded = jnp.concatenate([taps, jnp.zeros((1, 2 * tap_count), jnp.float32)], 1)
    spread = jnp.broadcast_to(padded, (2 * tap_count, 3 * tap_count))
    rolled = pltpu.roll(spread, 2 * tap_count + 1, 1, stride=1, stride_axis=0)
    table = rolled[:, :tap_count].astype(jnp.bfloat16)

    def window(part, block):
        return jnp.concatenate([halo_ref[part, block], fields_ref[part, block]], 1).astype(jnp.float32)

    def body(slot_index, carry):
        left = ints_ref[2 * slot_index]
        right = ints_ref[2 * slot_index + 1]
        left_real = window(0, left)[:, None]
        left_imag = window(1, left)[:, None]
        right_real = window(0, right)[None]
        right_imag = window(1, right)[None]
        real_part = (left_real * right_real + left_imag * right_imag).reshape(square, width)
        imag_part = (left_imag * right_real - left_real * right_imag).reshape(square, width)
        intensity = jnp.concatenate([real_part, imag_part], 0).astype(jnp.bfloat16)
        pieces = []
        for piece in range(length // tap_count):
            span = intensity[:, piece * tap_count:piece * tap_count + 2 * tap_count]
            pieces.append(jnp.dot(span, table, preferred_element_type=jnp.float32))
        response = jnp.concatenate(pieces, 1).astype(jnp.bfloat16)
        for entry_index in range(entries):
            matrix = values_ref[slot_index, entry_index]
            mixed_real = jnp.dot(matrix, response[:square], preferred_element_type=jnp.float32).reshape(
                block_size, block_size, length
            )
            mixed_imag = jnp.dot(matrix, response[square:], preferred_element_type=jnp.float32).reshape(
                block_size, block_size, length
            )
            light = ints_ref[light_base + entries * slot_index + entry_index]
            light_real = fields_ref[0, light].astype(jnp.float32)[None]
            light_imag = fields_ref[1, light].astype(jnp.float32)[None]
            out_real = jnp.sum(light_real * mixed_real - light_imag * mixed_imag, axis=1)
            out_imag = jnp.sum(light_real * mixed_imag + light_imag * mixed_real, axis=1)
            partials_ref[entries * slot_index + entry_index, 0] = out_real
            partials_ref[entries * slot_index + entry_index, 1] = out_imag
        return carry

    lax.fori_loop(0, slot_count, body, 0, unroll=True)

    def block_sum(peer, part):
        block = peer * owned + part
        first = ints_ref[pick_base + 2 * block]
        second = ints_ref[pick_base + 2 * block + 1]
        return partials_ref[first] + partials_ref[second]

    pl.semaphore_wait(barrier, pair_count - 1)

    def outgoing(peer):
        return pltpu.make_async_remote_copy(
            src_ref=send_ref.at[peer],
            dst_ref=recv_ref.at[me],
            send_sem=send_sems.at[peer],
            recv_sem=recv_sems.at[me],
            device_id=(row, peer),
            device_id_type=mesh_ids,
        )

    def send(step, carry):
        peer = lax.rem(me + step, pair_count)
        for part in range(owned):
            send_ref[peer, part] = block_sum(peer, part).astype(send_ref.dtype)
        outgoing(peer).start()
        return carry

    lax.fori_loop(1, pair_count, send, 0)

    def gather(step, total):
        peer = lax.rem(me + pair_count - step, pair_count)
        incoming = pltpu.make_async_remote_copy(
            src_ref=send_ref.at[peer],
            dst_ref=recv_ref.at[peer],
            send_sem=send_sems.at[peer],
            recv_sem=recv_sems.at[peer],
            device_id=(row, peer),
            device_id_type=mesh_ids,
        )
        incoming.wait_recv()
        return total + recv_ref[peer].astype(jnp.float32)

    own = jnp.stack([block_sum(me, part) for part in range(owned)])
    total = lax.fori_loop(1, pair_count, gather, own)

    def finish(step, carry):
        outgoing(lax.rem(me + step, pair_count)).wait_send()
        return carry

    lax.fori_loop(1, pair_count, finish, 0)
    out_ref[...] = total


def local(
    mode_fields, raman_taps, pair_blocks, light_blocks, target_blocks, raman_values, live_slots
):
    tap_count = raman_taps.shape[0]
    block_size = MB
    tm_count = lax.axis_size("tm")
    pair_count = lax.axis_size("pair")
    slot_count = pair_blocks.shape[1]
    entries = light_blocks.shape[2]
    mode_count = mode_fields.shape[1]
    length = mode_fields.shape[2]
    blocks = mode_count // block_size
    owned = blocks // pair_count
    rows = slot_count * entries
    halo = lax.ppermute(
        mode_fields[:, :, -tap_count:], "tm", [(k, k + 1) for k in range(tm_count - 1)]
    )
    halo = halo.reshape(2, blocks, block_size, tap_count)
    fields = mode_fields.reshape(2, blocks, block_size, length)
    square = block_size * block_size
    values = raman_values[0].reshape(slot_count, entries, square, square)
    row_index = jnp.arange(rows, dtype=jnp.int32)
    live_rows = row_index // entries < live_slots[0]
    feeds = (target_blocks.reshape(1, rows) == jnp.arange(blocks, dtype=jnp.int32)[:, None]) & live_rows[None]
    first = jnp.min(jnp.where(feeds, row_index[None], rows), axis=1)
    last = jnp.max(jnp.where(feeds, row_index[None], -1), axis=1)
    second = jnp.where(last > first, last, rows)
    ints = jnp.concatenate(
        [pair_blocks.reshape(-1), light_blocks.reshape(-1), jnp.stack([first, second], 1).reshape(-1)]
    )
    smem = pl.BlockSpec(memory_space=pltpu.SMEM)
    vmem = pl.BlockSpec(memory_space=pltpu.VMEM)
    exchange_shape = (pair_count, owned, 2, block_size, length)
    shared = pl.pallas_call(
        functools.partial(fused_kernel, slot_count, entries),
        out_shape=jax.ShapeDtypeStruct((owned, 2, block_size, length), jnp.float32),
        in_specs=[smem, vmem, vmem, vmem, vmem],
        out_specs=vmem,
        scratch_shapes=[
            pltpu.VMEM((rows + 1, 2, block_size, length), jnp.float32),
            pltpu.VMEM(exchange_shape, jnp.bfloat16),
            pltpu.VMEM(exchange_shape, jnp.bfloat16),
            pltpu.SemaphoreType.DMA((pair_count,)),
            pltpu.SemaphoreType.DMA((pair_count,)),
        ],
        compiler_params=pltpu.CompilerParams(collective_id=0, has_side_effects=True),
    )(ints, halo, fields, raman_taps.reshape(1, tap_count), values)
    result = jnp.transpose(shared, (1, 0, 2, 3)).reshape(2, owned * block_size, length)
    return result


def solution(mesh):
    return jax.shard_map(
        local,
        mesh=mesh,
        in_specs=(
            P(None, None, "tm"),
            P(),
            P("pair", None, None),
            P("pair", None, None),
            P("pair", None),
            P("pair", None, None, None),
            P("pair"),
        ),
        out_specs=P(None, "pair", "tm"),
        check_vma=False,
    )
```

```python
import functools

import jax
import jax.numpy as jnp
from jax import lax
from jax.sharding import PartitionSpec as P
from jax.experimental import pallas as pl
from jax.experimental.pallas import tpu as pltpu

MB = 8


def fused_kernel(
    slot_count, entries,
    ints_ref, halo_ref, fields_ref, table_ref, values_ref, out_ref,
    partials_ref, send_ref, recv_ref, send_sems, recv_sems,
):
    block_size = fields_ref.shape[2]
    length = fields_ref.shape[3]
    tap_count = halo_ref.shape[3]
    width = length + tap_count
    square = block_size * block_size
    pair_count = send_ref.shape[0]
    owned = send_ref.shape[1]
    light_base = 2 * slot_count
    pick_base = light_base + entries * slot_count
    zero_row = slot_count * entries
    me = lax.axis_index("pair")
    row = lax.axis_index("tm")
    mesh_ids = pl.DeviceIdType.MESH
    barrier = pltpu.get_barrier_semaphore()

    def greet(step, carry):
        peer = lax.rem(me + step, pair_count)
        pl.semaphore_signal(barrier, inc=1, device_id=(row, peer), device_id_type=mesh_ids)
        return carry

    lax.fori_loop(1, pair_count, greet, 0)

    partials_ref[zero_row] = jnp.zeros(partials_ref.shape[1:], partials_ref.dtype)
    tap_count = halo_ref.shape[3]
    period = (fields_ref.shape[3] + halo_ref.shape[3] + fields_ref.shape[3]) // tap_count * tap_count
    taps = table_ref[...].astype(jnp.float32)
    padded = jnp.concatenate([taps, jnp.zeros((1, period - tap_count), jnp.float32)], 1)
    spread = jnp.broadcast_to(padded, (fields_ref.shape[3] + tap_count, period))
    rolled = pltpu.roll(spread, period - tap_count + 1, 1, stride=1, stride_axis=0)
    table = rolled[:, :fields_ref.shape[3]].astype(jnp.bfloat16)

    def window(part, block):
        return jnp.concatenate([halo_ref[part, block], fields_ref[part, block]], 1).astype(jnp.float32)

    def body(slot_index, carry):
        left = ints_ref[2 * slot_index]
        right = ints_ref[2 * slot_index + 1]
        left_real = window(0, left)[:, None]
        left_imag = window(1, left)[:, None]
        right_real = window(0, right)[None]
        right_imag = window(1, right)[None]
        real_part = (left_real * right_real + left_imag * right_imag).reshape(square, width)
        imag_part = (left_imag * right_real - left_real * right_imag).reshape(square, width)
        intensity = jnp.concatenate([real_part, imag_part], 0).astype(jnp.bfloat16)
        response = jnp.dot(intensity, table, preferred_element_type=jnp.float32).astype(jnp.bfloat16)
        for entry_index in range(entries):
            matrix = values_ref[slot_index, entry_index]
            mixed_real = jnp.dot(matrix, response[:square], preferred_element_type=jnp.float32).reshape(
                block_size, block_size, length
            )
            mixed_imag = jnp.dot(matrix, response[square:], preferred_element_type=jnp.float32).reshape(
                block_size, block_size, length
            )
            light = ints_ref[light_base + entries * slot_index + entry_index]
            light_real = fields_ref[0, light].astype(jnp.float32)[None]
            light_imag = fields_ref[1, light].astype(jnp.float32)[None]
            out_real = jnp.sum(light_real * mixed_real - light_imag * mixed_imag, axis=1)
            out_imag = jnp.sum(light_real * mixed_imag + light_imag * mixed_real, axis=1)
            partials_ref[entries * slot_index + entry_index, 0] = out_real
            partials_ref[entries * slot_index + entry_index, 1] = out_imag
        return carry

    lax.fori_loop(0, slot_count, body, 0, unroll=True)

    def block_sum(peer, part):
        block = peer * owned + part
        first = ints_ref[pick_base + 2 * block]
        second = ints_ref[pick_base + 2 * block + 1]
        return partials_ref[first] + partials_ref[second]

    pl.semaphore_wait(barrier, pair_count - 1)

    def outgoing(peer):
        return pltpu.make_async_remote_copy(
            src_ref=send_ref.at[peer],
            dst_ref=recv_ref.at[me],
            send_sem=send_sems.at[peer],
            recv_sem=recv_sems.at[me],
            device_id=(row, peer),
            device_id_type=mesh_ids,
        )

    def send(step, carry):
        peer = lax.rem(me + step, pair_count)
        for part in range(owned):
            send_ref[peer, part] = block_sum(peer, part).astype(send_ref.dtype)
        outgoing(peer).start()
        return carry

    lax.fori_loop(1, pair_count, send, 0)

    def gather(step, total):
        peer = lax.rem(me + pair_count - step, pair_count)
        incoming = pltpu.make_async_remote_copy(
            src_ref=send_ref.at[peer],
            dst_ref=recv_ref.at[peer],
            send_sem=send_sems.at[peer],
            recv_sem=recv_sems.at[peer],
            device_id=(row, peer),
            device_id_type=mesh_ids,
        )
        incoming.wait_recv()
        return total + recv_ref[peer].astype(jnp.float32)

    own = jnp.stack([block_sum(me, part) for part in range(owned)])
    total = lax.fori_loop(1, pair_count, gather, own)

    def finish(step, carry):
        outgoing(lax.rem(me + step, pair_count)).wait_send()
        return carry

    lax.fori_loop(1, pair_count, finish, 0)
    out_ref[...] = total


def local(
    mode_fields, raman_taps, pair_blocks, light_blocks, target_blocks, raman_values, live_slots
):
    tap_count = raman_taps.shape[0]
    block_size = MB
    tm_count = lax.axis_size("tm")
    pair_count = lax.axis_size("pair")
    slot_count = pair_blocks.shape[1]
    entries = light_blocks.shape[2]
    mode_count = mode_fields.shape[1]
    length = mode_fields.shape[2]
    blocks = mode_count // block_size
    owned = blocks // pair_count
    rows = slot_count * entries
    halo = lax.ppermute(
        mode_fields[:, :, -tap_count:], "tm", [(k, k + 1) for k in range(tm_count - 1)]
    )
    halo = halo.reshape(2, blocks, block_size, tap_count)
    fields = mode_fields.reshape(2, blocks, block_size, length)
    square = block_size * block_size
    values = raman_values[0].reshape(slot_count, entries, square, square)
    row_index = jnp.arange(rows, dtype=jnp.int32)
    live_rows = row_index // entries < live_slots[0]
    feeds = (target_blocks.reshape(1, rows) == jnp.arange(blocks, dtype=jnp.int32)[:, None]) & live_rows[None]
    first = jnp.min(jnp.where(feeds, row_index[None], rows), axis=1)
    last = jnp.max(jnp.where(feeds, row_index[None], -1), axis=1)
    second = jnp.where(last > first, last, rows)
    ints = jnp.concatenate(
        [pair_blocks.reshape(-1), light_blocks.reshape(-1), jnp.stack([first, second], 1).reshape(-1)]
    )
    smem = pl.BlockSpec(memory_space=pltpu.SMEM)
    vmem = pl.BlockSpec(memory_space=pltpu.VMEM)
    exchange_shape = (pair_count, owned, 2, block_size, length)
    shared = pl.pallas_call(
        functools.partial(fused_kernel, slot_count, entries),
        out_shape=jax.ShapeDtypeStruct((owned, 2, block_size, length), jnp.float32),
        in_specs=[smem, vmem, vmem, vmem, vmem],
        out_specs=vmem,
        scratch_shapes=[
            pltpu.VMEM((rows + 1, 2, block_size, length), jnp.float32),
            pltpu.VMEM(exchange_shape, jnp.bfloat16),
            pltpu.VMEM(exchange_shape, jnp.bfloat16),
            pltpu.SemaphoreType.DMA((pair_count,)),
            pltpu.SemaphoreType.DMA((pair_count,)),
        ],
        compiler_params=pltpu.CompilerParams(collective_id=0, has_side_effects=True),
    )(ints, halo, fields, raman_taps.reshape(1, tap_count), values)
    result = jnp.transpose(shared, (1, 0, 2, 3)).reshape(2, owned * block_size, length)
    return result


def solution(mesh):
    return jax.shard_map(
        local,
        mesh=mesh,
        in_specs=(
            P(None, None, "tm"),
            P(),
            P("pair", None, None),
            P("pair", None, None),
            P("pair", None),
            P("pair", None, None, None),
            P("pair"),
        ),
        out_specs=P(None, "pair", "tm"),
        check_vma=False,
    )
```

```python
import functools

import jax
import jax.numpy as jnp
from jax import lax
from jax.sharding import PartitionSpec as P
from jax.experimental import pallas as pl
from jax.experimental.pallas import tpu as pltpu

MB = 8


def fused_kernel(
    slot_count, entries,
    ints_ref, halo_ref, fields_ref, table_ref, values_ref, out_ref,
    partials_ref, send_ref, recv_ref, send_sems, recv_sems,
):
    block_size = fields_ref.shape[2]
    length = fields_ref.shape[3]
    tap_count = halo_ref.shape[3]
    width = length + tap_count
    square = block_size * block_size
    pair_count = send_ref.shape[0]
    owned = send_ref.shape[1]
    light_base = 2 * slot_count
    pick_base = light_base + entries * slot_count
    zero_row = slot_count * entries
    me = lax.axis_index("pair")
    row = lax.axis_index("tm")
    mesh_ids = pl.DeviceIdType.MESH
    barrier = pltpu.get_barrier_semaphore()

    def greet(step, carry):
        peer = lax.rem(me + step, pair_count)
        pl.semaphore_signal(barrier, inc=1, device_id=(row, peer), device_id_type=mesh_ids)
        return carry

    lax.fori_loop(1, pair_count, greet, 0)

    partials_ref[zero_row] = jnp.zeros(partials_ref.shape[1:], partials_ref.dtype)
    tap_count = halo_ref.shape[3]
    taps = table_ref[...].astype(jnp.float32)
    padded = jnp.concatenate([taps, jnp.zeros((1, 2 * tap_count), jnp.float32)], 1)
    spread = jnp.broadcast_to(padded, (2 * tap_count, 3 * tap_count))
    rolled = pltpu.roll(spread, 2 * tap_count + 1, 1, stride=1, stride_axis=0)
    table = rolled[:, :tap_count].astype(jnp.bfloat16)

    def window(part, block):
        return jnp.concatenate([halo_ref[part, block], fields_ref[part, block]], 1).astype(jnp.float32)

    def body(slot_index, carry):
        left = ints_ref[2 * slot_index]
        right = ints_ref[2 * slot_index + 1]
        left_real = window(0, left)[:, None]
        left_imag = window(1, left)[:, None]
        right_real = window(0, right)[None]
        right_imag = window(1, right)[None]
        real_part = (left_real * right_real + left_imag * right_imag).reshape(square, width)
        imag_part = (left_imag * right_real - left_real * right_imag).reshape(square, width)
        intensity = jnp.concatenate([real_part, imag_part], 0).astype(jnp.bfloat16)
        pieces = []
        for piece in range(length // tap_count):
            span = intensity[:, piece * tap_count:piece * tap_count + 2 * tap_count]
            pieces.append(jnp.dot(span, table, preferred_element_type=jnp.float32))
        response = jnp.concatenate(pieces, 1).astype(jnp.bfloat16)
        matrices = values_ref[slot_index].reshape(entries * square, square)
        sides = jnp.concatenate([response[:square], response[square:]], 1)
        mixed = jnp.dot(matrices, sides, preferred_element_type=jnp.float32)
        for entry_index in range(entries):
            rows = mixed[entry_index * square:(entry_index + 1) * square]
            mixed_real = rows[:, :length].reshape(block_size, block_size, length)
            mixed_imag = rows[:, length:].reshape(block_size, block_size, length)
            light = ints_ref[light_base + entries * slot_index + entry_index]
            light_real = fields_ref[0, light].astype(jnp.float32)[None]
            light_imag = fields_ref[1, light].astype(jnp.float32)[None]
            out_real = jnp.sum(light_real * mixed_real - light_imag * mixed_imag, axis=1)
            out_imag = jnp.sum(light_real * mixed_imag + light_imag * mixed_real, axis=1)
            partials_ref[entries * slot_index + entry_index, 0] = out_real
            partials_ref[entries * slot_index + entry_index, 1] = out_imag
        return carry

    lax.fori_loop(0, slot_count, body, 0, unroll=True)

    def block_sum(peer, part):
        block = peer * owned + part
        first = ints_ref[pick_base + 2 * block]
        second = ints_ref[pick_base + 2 * block + 1]
        return partials_ref[first] + partials_ref[second]

    pl.semaphore_wait(barrier, pair_count - 1)

    def outgoing(peer):
        return pltpu.make_async_remote_copy(
            src_ref=send_ref.at[peer],
            dst_ref=recv_ref.at[me],
            send_sem=send_sems.at[peer],
            recv_sem=recv_sems.at[me],
            device_id=(row, peer),
            device_id_type=mesh_ids,
        )

    def send(step, carry):
        peer = lax.rem(me + step, pair_count)
        for part in range(owned):
            send_ref[peer, part] = block_sum(peer, part).astype(send_ref.dtype)
        outgoing(peer).start()
        return carry

    lax.fori_loop(1, pair_count, send, 0)

    def gather(step, total):
        peer = lax.rem(me + pair_count - step, pair_count)
        incoming = pltpu.make_async_remote_copy(
            src_ref=send_ref.at[peer],
            dst_ref=recv_ref.at[peer],
            send_sem=send_sems.at[peer],
            recv_sem=recv_sems.at[peer],
            device_id=(row, peer),
            device_id_type=mesh_ids,
        )
        incoming.wait_recv()
        return total + recv_ref[peer].astype(jnp.float32)

    own = jnp.stack([block_sum(me, part) for part in range(owned)])
    total = lax.fori_loop(1, pair_count, gather, own)

    def finish(step, carry):
        outgoing(lax.rem(me + step, pair_count)).wait_send()
        return carry

    lax.fori_loop(1, pair_count, finish, 0)
    out_ref[...] = total


def local(
    mode_fields, raman_taps, pair_blocks, light_blocks, target_blocks, raman_values, live_slots
):
    tap_count = raman_taps.shape[0]
    block_size = MB
    tm_count = lax.axis_size("tm")
    pair_count = lax.axis_size("pair")
    slot_count = pair_blocks.shape[1]
    entries = light_blocks.shape[2]
    mode_count = mode_fields.shape[1]
    length = mode_fields.shape[2]
    blocks = mode_count // block_size
    owned = blocks // pair_count
    rows = slot_count * entries
    halo = lax.ppermute(
        mode_fields[:, :, -tap_count:], "tm", [(k, k + 1) for k in range(tm_count - 1)]
    )
    halo = halo.reshape(2, blocks, block_size, tap_count)
    fields = mode_fields.reshape(2, blocks, block_size, length)
    square = block_size * block_size
    values = raman_values[0].reshape(slot_count, entries, square, square)
    row_index = jnp.arange(rows, dtype=jnp.int32)
    live_rows = row_index // entries < live_slots[0]
    feeds = (target_blocks.reshape(1, rows) == jnp.arange(blocks, dtype=jnp.int32)[:, None]) & live_rows[None]
    first = jnp.min(jnp.where(feeds, row_index[None], rows), axis=1)
    last = jnp.max(jnp.where(feeds, row_index[None], -1), axis=1)
    second = jnp.where(last > first, last, rows)
    ints = jnp.concatenate(
        [pair_blocks.reshape(-1), light_blocks.reshape(-1), jnp.stack([first, second], 1).reshape(-1)]
    )
    smem = pl.BlockSpec(memory_space=pltpu.SMEM)
    vmem = pl.BlockSpec(memory_space=pltpu.VMEM)
    exchange_shape = (pair_count, owned, 2, block_size, length)
    shared = pl.pallas_call(
        functools.partial(fused_kernel, slot_count, entries),
        out_shape=jax.ShapeDtypeStruct((owned, 2, block_size, length), jnp.float32),
        in_specs=[smem, vmem, vmem, vmem, vmem],
        out_specs=vmem,
        scratch_shapes=[
            pltpu.VMEM((rows + 1, 2, block_size, length), jnp.float32),
            pltpu.VMEM(exchange_shape, jnp.bfloat16),
            pltpu.VMEM(exchange_shape, jnp.bfloat16),
            pltpu.SemaphoreType.DMA((pair_count,)),
            pltpu.SemaphoreType.DMA((pair_count,)),
        ],
        compiler_params=pltpu.CompilerParams(collective_id=0, has_side_effects=True),
    )(ints, halo, fields, raman_taps.reshape(1, tap_count), values)
    result = jnp.transpose(shared, (1, 0, 2, 3)).reshape(2, owned * block_size, length)
    return result


def solution(mesh):
    return jax.shard_map(
        local,
        mesh=mesh,
        in_specs=(
            P(None, None, "tm"),
            P(),
            P("pair", None, None),
            P("pair", None, None),
            P("pair", None),
            P("pair", None, None, None),
            P("pair"),
        ),
        out_specs=P(None, "pair", "tm"),
        check_vma=False,
    )
```

```python
import functools

import jax
import jax.numpy as jnp
from jax import lax
from jax.sharding import PartitionSpec as P
from jax.experimental import pallas as pl
from jax.experimental.pallas import tpu as pltpu

MB = 8


def fused_kernel(
    slot_count, entries,
    ints_ref, halo_hbm, fields_ref, table_ref, values_ref, out_ref,
    partials_ref, send_ref, recv_ref, send_sems, recv_sems, halo_ref, halo_sem,
):
    block_size = fields_ref.shape[2]
    length = fields_ref.shape[3]
    tap_count = halo_ref.shape[3]
    width = length + tap_count
    square = block_size * block_size
    pair_count = send_ref.shape[0]
    owned = send_ref.shape[1]
    light_base = 2 * slot_count
    pick_base = light_base + entries * slot_count
    zero_row = slot_count * entries
    me = lax.axis_index("pair")
    row = lax.axis_index("tm")
    mesh_ids = pl.DeviceIdType.MESH
    barrier = pltpu.get_barrier_semaphore()

    def greet(step, carry):
        peer = lax.rem(me + step, pair_count)
        pl.semaphore_signal(barrier, inc=1, device_id=(row, peer), device_id_type=mesh_ids)
        return carry

    halo_copy = pltpu.make_async_copy(halo_hbm, halo_ref, halo_sem)
    halo_copy.start()
    lax.fori_loop(1, pair_count, greet, 0)
    halo_copy.wait()

    partials_ref[zero_row] = jnp.zeros(partials_ref.shape[1:], partials_ref.dtype)
    tap_count = halo_ref.shape[3]
    taps = table_ref[...].astype(jnp.float32)
    padded = jnp.concatenate([taps, jnp.zeros((1, 2 * tap_count), jnp.float32)], 1)
    spread = jnp.broadcast_to(padded, (2 * tap_count, 3 * tap_count))
    rolled = pltpu.roll(spread, 2 * tap_count + 1, 1, stride=1, stride_axis=0)
    table = rolled[:, :tap_count].astype(jnp.bfloat16)

    def window(part, block):
        return jnp.concatenate([halo_ref[part, block], fields_ref[part, block]], 1).astype(jnp.float32)

    def body(slot_index, carry):
        left = ints_ref[2 * slot_index]
        right = ints_ref[2 * slot_index + 1]
        left_real = window(0, left)[:, None]
        left_imag = window(1, left)[:, None]
        right_real = window(0, right)[None]
        right_imag = window(1, right)[None]
        real_part = (left_real * right_real + left_imag * right_imag).reshape(square, width)
        imag_part = (left_imag * right_real - left_real * right_imag).reshape(square, width)
        intensity = jnp.concatenate([real_part, imag_part], 0).astype(jnp.bfloat16)
        pieces = []
        for piece in range(length // tap_count):
            span = intensity[:, piece * tap_count:piece * tap_count + 2 * tap_count]
            pieces.append(jnp.dot(span, table, preferred_element_type=jnp.float32))
        response = jnp.concatenate(pieces, 1).astype(jnp.bfloat16)
        for entry_index in range(entries):
            matrix = values_ref[slot_index, entry_index]
            mixed_real = jnp.dot(matrix, response[:square], preferred_element_type=jnp.float32).reshape(
                block_size, block_size, length
            )
            mixed_imag = jnp.dot(matrix, response[square:], preferred_element_type=jnp.float32).reshape(
                block_size, block_size, length
            )
            light = ints_ref[light_base + entries * slot_index + entry_index]
            light_real = fields_ref[0, light].astype(jnp.float32)[None]
            light_imag = fields_ref[1, light].astype(jnp.float32)[None]
            out_real = jnp.sum(light_real * mixed_real - light_imag * mixed_imag, axis=1)
            out_imag = jnp.sum(light_real * mixed_imag + light_imag * mixed_real, axis=1)
            partials_ref[entries * slot_index + entry_index, 0] = out_real
            partials_ref[entries * slot_index + entry_index, 1] = out_imag
        return carry

    lax.fori_loop(0, slot_count, body, 0, unroll=True)

    def block_sum(peer, part):
        block = peer * owned + part
        first = ints_ref[pick_base + 2 * block]
        second = ints_ref[pick_base + 2 * block + 1]
        return partials_ref[first] + partials_ref[second]

    pl.semaphore_wait(barrier, pair_count - 1)

    def outgoing(peer):
        return pltpu.make_async_remote_copy(
            src_ref=send_ref.at[peer],
            dst_ref=recv_ref.at[me],
            send_sem=send_sems.at[peer],
            recv_sem=recv_sems.at[me],
            device_id=(row, peer),
            device_id_type=mesh_ids,
        )

    def send(step, carry):
        peer = lax.rem(me + step, pair_count)
        for part in range(owned):
            send_ref[peer, part] = block_sum(peer, part).astype(send_ref.dtype)
        outgoing(peer).start()
        return carry

    lax.fori_loop(1, pair_count, send, 0)

    def gather(step, total):
        peer = lax.rem(me + pair_count - step, pair_count)
        incoming = pltpu.make_async_remote_copy(
            src_ref=send_ref.at[peer],
            dst_ref=recv_ref.at[peer],
            send_sem=send_sems.at[peer],
            recv_sem=recv_sems.at[peer],
            device_id=(row, peer),
            device_id_type=mesh_ids,
        )
        incoming.wait_recv()
        return total + recv_ref[peer].astype(jnp.float32)

    own = jnp.stack([block_sum(me, part) for part in range(owned)])
    total = lax.fori_loop(1, pair_count, gather, own)

    def finish(step, carry):
        outgoing(lax.rem(me + step, pair_count)).wait_send()
        return carry

    lax.fori_loop(1, pair_count, finish, 0)
    out_ref[...] = total


def local(
    mode_fields, raman_taps, pair_blocks, light_blocks, target_blocks, raman_values, live_slots
):
    tap_count = raman_taps.shape[0]
    block_size = MB
    tm_count = lax.axis_size("tm")
    pair_count = lax.axis_size("pair")
    slot_count = pair_blocks.shape[1]
    entries = light_blocks.shape[2]
    mode_count = mode_fields.shape[1]
    length = mode_fields.shape[2]
    blocks = mode_count // block_size
    owned = blocks // pair_count
    rows = slot_count * entries
    halo = lax.ppermute(
        mode_fields[:, :, -tap_count:], "tm", [(k, k + 1) for k in range(tm_count - 1)]
    )
    halo = halo.reshape(2, blocks, block_size, tap_count)
    fields = mode_fields.reshape(2, blocks, block_size, length)
    square = block_size * block_size
    values = raman_values[0].reshape(slot_count, entries, square, square)
    row_index = jnp.arange(rows, dtype=jnp.int32)
    live_rows = row_index // entries < live_slots[0]
    feeds = (target_blocks.reshape(1, rows) == jnp.arange(blocks, dtype=jnp.int32)[:, None]) & live_rows[None]
    first = jnp.min(jnp.where(feeds, row_index[None], rows), axis=1)
    last = jnp.max(jnp.where(feeds, row_index[None], -1), axis=1)
    second = jnp.where(last > first, last, rows)
    ints = jnp.concatenate(
        [pair_blocks.reshape(-1), light_blocks.reshape(-1), jnp.stack([first, second], 1).reshape(-1)]
    )
    smem = pl.BlockSpec(memory_space=pltpu.SMEM)
    vmem = pl.BlockSpec(memory_space=pltpu.VMEM)
    exchange_shape = (pair_count, owned, 2, block_size, length)
    shared = pl.pallas_call(
        functools.partial(fused_kernel, slot_count, entries),
        out_shape=jax.ShapeDtypeStruct((owned, 2, block_size, length), jnp.float32),
        in_specs=[smem, pl.BlockSpec(memory_space=pl.ANY), vmem, vmem, vmem],
        out_specs=vmem,
        scratch_shapes=[
            pltpu.VMEM((rows + 1, 2, block_size, length), jnp.float32),
            pltpu.VMEM(exchange_shape, jnp.bfloat16),
            pltpu.VMEM(exchange_shape, jnp.bfloat16),
            pltpu.SemaphoreType.DMA((pair_count,)),
            pltpu.SemaphoreType.DMA((pair_count,)),
            pltpu.VMEM((2, blocks, block_size, tap_count), mode_fields.dtype),
            pltpu.SemaphoreType.DMA(()),
        ],
        compiler_params=pltpu.CompilerParams(collective_id=0, has_side_effects=True),
    )(ints, halo, fields, raman_taps.reshape(1, tap_count), values)
    result = jnp.transpose(shared, (1, 0, 2, 3)).reshape(2, owned * block_size, length)
    return result


def solution(mesh):
    return jax.shard_map(
        local,
        mesh=mesh,
        in_specs=(
            P(None, None, "tm"),
            P(),
            P("pair", None, None),
            P("pair", None, None),
            P("pair", None),
            P("pair", None, None, None),
            P("pair"),
        ),
        out_specs=P(None, "pair", "tm"),
        check_vma=False,
    )
```

```python
import functools

import jax
import jax.numpy as jnp
from jax import lax
from jax.sharding import PartitionSpec as P
from jax.experimental import pallas as pl
from jax.experimental.pallas import tpu as pltpu

MB = 8
Y_IN_PAIR = 4


def fused_kernel(
    slot_count, entries,
    ints_ref, halo_ref, fields_ref, table_ref, values_ref, out_ref,
    partials_ref, send_ref, recv_ref, send_sems, recv_sems,
):
    block_size = fields_ref.shape[2]
    length = fields_ref.shape[3]
    tap_count = halo_ref.shape[3]
    width = length + tap_count
    square = block_size * block_size
    pair_count = send_ref.shape[0]
    owned = send_ref.shape[1]
    light_base = 2 * slot_count
    pick_base = light_base + entries * slot_count
    zero_row = slot_count * entries
    me = lax.axis_index("pair")
    row = lax.axis_index("tm")
    mesh_ids = pl.DeviceIdType.MESH
    barrier = pltpu.get_barrier_semaphore()

    def greet(step, carry):
        peer = lax.rem(me + step, pair_count)
        pl.semaphore_signal(barrier, inc=1, device_id=(row, peer), device_id_type=mesh_ids)
        return carry

    lax.fori_loop(1, pair_count, greet, 0)

    partials_ref[zero_row] = jnp.zeros(partials_ref.shape[1:], partials_ref.dtype)
    tap_count = halo_ref.shape[3]
    taps = table_ref[...].astype(jnp.float32)
    padded = jnp.concatenate([taps, jnp.zeros((1, 2 * tap_count), jnp.float32)], 1)
    spread = jnp.broadcast_to(padded, (2 * tap_count, 3 * tap_count))
    rolled = pltpu.roll(spread, 2 * tap_count + 1, 1, stride=1, stride_axis=0)
    table = rolled[:, :tap_count].astype(jnp.bfloat16)

    def window(part, block):
        return jnp.concatenate([halo_ref[part, block], fields_ref[part, block]], 1).astype(jnp.float32)

    def body(slot_index, carry):
        left = ints_ref[2 * slot_index]
        right = ints_ref[2 * slot_index + 1]
        left_real = window(0, left)[:, None]
        left_imag = window(1, left)[:, None]
        right_real = window(0, right)[None]
        right_imag = window(1, right)[None]
        real_part = (left_real * right_real + left_imag * right_imag).reshape(square, width)
        imag_part = (left_imag * right_real - left_real * right_imag).reshape(square, width)
        intensity = jnp.concatenate([real_part, imag_part], 0).astype(jnp.bfloat16)
        pieces = []
        for piece in range(length // tap_count):
            span = intensity[:, piece * tap_count:piece * tap_count + 2 * tap_count]
            pieces.append(jnp.dot(span, table, preferred_element_type=jnp.float32))
        response = jnp.concatenate(pieces, 1).astype(jnp.bfloat16)
        for entry_index in range(entries):
            matrix = values_ref[slot_index, entry_index]
            mixed_real = jnp.dot(matrix, response[:square], preferred_element_type=jnp.float32).reshape(
                block_size, block_size, length
            )
            mixed_imag = jnp.dot(matrix, response[square:], preferred_element_type=jnp.float32).reshape(
                block_size, block_size, length
            )
            light = ints_ref[light_base + entries * slot_index + entry_index]
            light_real = fields_ref[0, light].astype(jnp.float32)[None]
            light_imag = fields_ref[1, light].astype(jnp.float32)[None]
            out_real = jnp.sum(light_real * mixed_real - light_imag * mixed_imag, axis=1)
            out_imag = jnp.sum(light_real * mixed_imag + light_imag * mixed_real, axis=1)
            partials_ref[entries * slot_index + entry_index, 0] = out_real
            partials_ref[entries * slot_index + entry_index, 1] = out_imag
        return carry

    lax.fori_loop(0, slot_count, body, 0, unroll=True)

    def block_sum(peer, part):
        block = peer * owned + part
        first = ints_ref[pick_base + 2 * block]
        second = ints_ref[pick_base + 2 * block + 1]
        return partials_ref[first] + partials_ref[second]

    pl.semaphore_wait(barrier, pair_count - 1)

    def outgoing(peer):
        return pltpu.make_async_remote_copy(
            src_ref=send_ref.at[peer],
            dst_ref=recv_ref.at[me],
            send_sem=send_sems.at[peer],
            recv_sem=recv_sems.at[me],
            device_id=(row, peer),
            device_id_type=mesh_ids,
        )

    y_count = Y_IN_PAIR
    z_count = pair_count // y_count
    my_y = lax.rem(me, y_count)
    my_z = me // y_count

    def hops(offset):
        dz, dy = offset
        return min(dz, z_count - dz) + min(dy, y_count - dy)

    offsets = [(dz, dy) for dz in range(z_count) for dy in range(y_count) if (dz, dy) != (0, 0)]
    for dz, dy in sorted(offsets, key=lambda offset: -hops(offset)):
        peer = lax.rem(my_z + dz, z_count) * y_count + lax.rem(my_y + dy, y_count)
        for part in range(owned):
            send_ref[peer, part] = block_sum(peer, part).astype(send_ref.dtype)
        outgoing(peer).start()

    def gather(step, total):
        peer = lax.rem(me + pair_count - step, pair_count)
        incoming = pltpu.make_async_remote_copy(
            src_ref=send_ref.at[peer],
            dst_ref=recv_ref.at[peer],
            send_sem=send_sems.at[peer],
            recv_sem=recv_sems.at[peer],
            device_id=(row, peer),
            device_id_type=mesh_ids,
        )
        incoming.wait_recv()
        return total + recv_ref[peer].astype(jnp.float32)

    own = jnp.stack([block_sum(me, part) for part in range(owned)])
    total = lax.fori_loop(1, pair_count, gather, own)

    def finish(step, carry):
        outgoing(lax.rem(me + step, pair_count)).wait_send()
        return carry

    lax.fori_loop(1, pair_count, finish, 0)
    out_ref[...] = total


def local(
    mode_fields, raman_taps, pair_blocks, light_blocks, target_blocks, raman_values, live_slots
):
    tap_count = raman_taps.shape[0]
    block_size = MB
    tm_count = lax.axis_size("tm")
    pair_count = lax.axis_size("pair")
    slot_count = pair_blocks.shape[1]
    entries = light_blocks.shape[2]
    mode_count = mode_fields.shape[1]
    length = mode_fields.shape[2]
    blocks = mode_count // block_size
    owned = blocks // pair_count
    rows = slot_count * entries
    halo = lax.ppermute(
        mode_fields[:, :, -tap_count:], "tm", [(k, k + 1) for k in range(tm_count - 1)]
    )
    halo = halo.reshape(2, blocks, block_size, tap_count)
    fields = mode_fields.reshape(2, blocks, block_size, length)
    square = block_size * block_size
    values = raman_values[0].reshape(slot_count, entries, square, square)
    row_index = jnp.arange(rows, dtype=jnp.int32)
    live_rows = row_index // entries < live_slots[0]
    feeds = (target_blocks.reshape(1, rows) == jnp.arange(blocks, dtype=jnp.int32)[:, None]) & live_rows[None]
    first = jnp.min(jnp.where(feeds, row_index[None], rows), axis=1)
    last = jnp.max(jnp.where(feeds, row_index[None], -1), axis=1)
    second = jnp.where(last > first, last, rows)
    ints = jnp.concatenate(
        [pair_blocks.reshape(-1), light_blocks.reshape(-1), jnp.stack([first, second], 1).reshape(-1)]
    )
    smem = pl.BlockSpec(memory_space=pltpu.SMEM)
    vmem = pl.BlockSpec(memory_space=pltpu.VMEM)
    exchange_shape = (pair_count, owned, 2, block_size, length)
    shared = pl.pallas_call(
        functools.partial(fused_kernel, slot_count, entries),
        out_shape=jax.ShapeDtypeStruct((owned, 2, block_size, length), jnp.float32),
        in_specs=[smem, vmem, vmem, vmem, vmem],
        out_specs=vmem,
        scratch_shapes=[
            pltpu.VMEM((rows + 1, 2, block_size, length), jnp.float32),
            pltpu.VMEM(exchange_shape, jnp.bfloat16),
            pltpu.VMEM(exchange_shape, jnp.bfloat16),
            pltpu.SemaphoreType.DMA((pair_count,)),
            pltpu.SemaphoreType.DMA((pair_count,)),
        ],
        compiler_params=pltpu.CompilerParams(collective_id=0, has_side_effects=True),
    )(ints, halo, fields, raman_taps.reshape(1, tap_count), values)
    result = jnp.transpose(shared, (1, 0, 2, 3)).reshape(2, owned * block_size, length)
    return result


def solution(mesh):
    return jax.shard_map(
        local,
        mesh=mesh,
        in_specs=(
            P(None, None, "tm"),
            P(),
            P("pair", None, None),
            P("pair", None, None),
            P("pair", None),
            P("pair", None, None, None),
            P("pair"),
        ),
        out_specs=P(None, "pair", "tm"),
        check_vma=False,
    )
```
